32 devices in a mesh: slab: 2 (over y), gy: 4 (over z), gx: 4 (over x, core).
Axes of the slice: x: 2, y: 2, z: 4, core: 2. Of those that a mesh axis runs over, the one named last changes fastest.
Arguments:
- volume: float32 [8, 256, 1024], P(None, ('slab', 'gy'), 'gx'), parts along dimension 1, may hold values from -8 to 8
- tissue_mask: int32 [2, 32, 128], P(None, ('slab', 'gy'), 'gx'), parts along dimension 1, may hold values from 0 to 1
- smoothing: float32 [1], replicated, may hold values from 0.7 to 1.4
Outputs:
- filtered: float32 [8, 256, 1024], P(None, ('slab', 'gy'), 'gx'), parts along dimension 1
The draws below stay inside these ranges and needn't reach their ends.
There are 2 independent parts, one for each index of `slab`. The reference program is written for one: setup_inputs(seed, part) draws one part's arguments, and reference() takes and returns one part's arrays. A program takes and returns all parts, laid end to end along the dimension named above; an argument that names none is the same for every part. Nothing has to cross between parts.
All inputs are finite; a program needn't handle non-finite values.
Results may differ from the reference program's by a relative error of at most 0.00002.
Values sent between devices are 32-bit elements; how exact they have to be, the bound alone decides.
A program may use at most 64 MiB of HBM per device.

```python
import jax
import jax.numpy as jnp

Z = 8
ITERS = 2
NY = 128
NX = 1024


def draw_volume(key, part):
    first_key = jax.random.fold_in(key, 11)
    second_key = jax.random.fold_in(key, 12)
    rows_pos = jnp.arange(NY).astype(jnp.float32)
    row_scale = jnp.exp(jnp.log(3.0) * rows_pos / (NY - 1))[None, :, None]
    levels = 1.5 * jax.random.normal(second_key, (Z // 4, NY // 8, NX // 8), jnp.float32)
    spread = jnp.broadcast_to(levels[:, None, :, None, :, None], (Z // 4, 4, NY // 8, 8, NX // 8, 8)).reshape(Z, NY, NX)
    noise = jax.random.normal(first_key, (Z, NY, NX), jnp.float32)
    result = spread + noise * row_scale
    return jnp.clip(result, -8.0, 8.0)


def draw_tissue_mask(key, part):
    mask_key = jax.random.fold_in(key, 21)
    rolls = jax.random.randint(mask_key, (Z // 4, NY // 8, NX // 8), 0, 1000)
    rows_pos = jnp.arange(NY // 8)
    limits = 300 + 600 * rows_pos // max(NY // 8 - 1, 1)
    return (rolls < limits[None, :, None]).astype(jnp.int32)


def setup_inputs(seed: int = 0, part: int = 0) -> dict:
    seeds = jax.random.split(jax.random.key(seed), 4)
    part_splits = jax.random.split(jax.random.fold_in(seeds[3], part), 4)
    return {
        "volume": draw_volume(jax.random.fold_in(jax.random.fold_in(seeds[3], part), 71), part),
        "tissue_mask": draw_tissue_mask(jax.random.fold_in(jax.random.fold_in(seeds[3], part), 71), part),
        "smoothing": jnp.clip(jax.random.uniform(seeds[2], (1,), jnp.float32, 0.7, 1.4), 0.7, 1.4),
    }


OFFSETS = [(a, b, c) for a in (-4, 0, 4) for b in (-8, 0, 8) for c in (-8, 0, 8)]


def expand_mask(tissue_mask):
    blocks_z, blocks_y, blocks_x = tissue_mask.shape
    spread = jnp.broadcast_to(tissue_mask[:, None, :, None, :, None], (blocks_z, 4, blocks_y, 8, blocks_x, 8))
    return spread.reshape(blocks_z * 4, blocks_y * 8, blocks_x * 8).astype(jnp.float32)


def noise_terms(values, tissue):
    residual = values[1:-1] - 0.5 * (values[:-2] + values[2:])
    inner = tissue[1:-1]
    summed = jnp.sum(inner * residual * residual) * (2.0 / 3.0)
    return summed, jnp.sum(inner)


def box_sum(squared, depth, rows, cols):
    first = squared[0:depth] + squared[1:depth + 1] + squared[2:depth + 2]
    second = first[:, 0:rows] + first[:, 1:rows + 1] + first[:, 2:rows + 2]
    return second[:, :, 0:cols] + second[:, :, 1:cols + 1] + second[:, :, 2:cols + 2]


def smooth_once(padded_vals, padded_tiss, values, tissue, inverse_width):
    depth, rows, cols = values.shape
    centre = padded_vals[4:depth + 6, 8:rows + 10, 8:cols + 10]
    numerator = jnp.zeros(values.shape, jnp.float32)
    denominator = jnp.zeros(values.shape, jnp.float32)
    for offset in OFFSETS:
        shift_z, shift_y, shift_x = offset
        moved = padded_vals[4 + shift_z:depth + 6 + shift_z, 8 + shift_y:rows + 10 + shift_y, 8 + shift_x:cols + 10 + shift_x]
        differ = centre - moved
        distance = box_sum(differ * differ, depth, rows, cols)
        other_tiss = padded_tiss[5 + shift_z:5 + shift_z + depth, 9 + shift_y:9 + shift_y + rows, 9 + shift_x:9 + shift_x + cols]
        other_vals = padded_vals[5 + shift_z:5 + shift_z + depth, 9 + shift_y:9 + shift_y + rows, 9 + shift_x:9 + shift_x + cols]
        weight_field = jnp.exp(-distance * inverse_width) * other_tiss
        numerator = numerator + weight_field * other_vals
        denominator = denominator + weight_field
    return tissue * numerator / (denominator + 1.0 - tissue) + (1.0 - tissue) * values


def reference(volume, tissue_mask, smoothing):
    tissue = expand_mask(tissue_mask)
    summed, tissue_count = noise_terms(volume, tissue)
    variance = summed / jnp.maximum(tissue_count, 1.0) + 1e-5
    inverse_width = 1.0 / (54.0 * smoothing[0] * smoothing[0] * variance)
    widths = ((5, 5), (9, 9), (9, 9))
    padded_tiss = jnp.pad(tissue, widths)
    values = volume
    for iteration in range(ITERS):
        padded_vals = jnp.pad(values, widths)
        values = smooth_once(padded_vals, padded_tiss, values, tissue, inverse_width)
    return values
```

```python
import functools

import jax
import jax.numpy as jnp
from jax import lax
from jax.experimental import pallas as pl
from jax.experimental.pallas import tpu as pltpu
from jax.sharding import PartitionSpec as P

MESH = pl.DeviceIdType.MESH
ITERS = 2
LOG2E = 1.4426950408889634
BIG = 1e30
DIRS = ((1, 0), (-1, 0), (0, 1), (0, -1), (1, 1), (1, -1), (-1, 1), (-1, -1))
LEVEL = ((0, 0, 8), (0, 8, 8), (0, -8, 8), (0, 8, 0))
CROSS = (
    (4, 0, 8), (4, 8, 8), (4, -8, 8), (-4, 0, 8), (-4, 8, 8), (-4, -8, 8), (4, 0, 0), (4, 8, 0), (4, -8, 0)
)
PAD = 16
SLOTS = 32


def kernel(
    ny, nx, smooth_ref, vol_hbm, mask_hbm, out_ref, vol_ref, mask_ref, mid, vals, packs, squares,
    cubes, acc, pacc, pens, ppens, own_tiss, near_tiss, wide_tiss,
    rows_in, row_in, row_out, pack_out, pack_in, side_in, corner_in, sums,
    load_sem, sum_send, sum_recv, halo_send, halo_recv,
):
    depth, rows, cols = vol_ref.shape
    lanes = 128
    blocks_z, blocks_y, blocks_x = mask_ref.shape
    nb = rows // 8
    step = lanes - 2
    peers = ny * nx
    gy, gx = lax.axis_index("gy"), lax.axis_index("gx")
    me = gy * nx + gx

    barrier = pltpu.get_barrier_semaphore()
    for k in range(1, peers):
        flat = lax.rem(me + k, peers)
        pl.semaphore_signal(
            barrier, inc=1, device_id={"gy": flat // nx, "gx": lax.rem(flat, nx)}, device_id_type=MESH
        )

    loads = [
        pltpu.make_async_copy(mask_hbm, mask_ref, load_sem.at[0]),
        pltpu.make_async_copy(vol_hbm, vol_ref, load_sem.at[1]),
    ]
    for load in loads:
        load.start()

    def lane_of(n):
        return lax.broadcasted_iota(jnp.int32, (n, lanes), 1)

    def exists(dy, dx):
        found = None
        for move, pos, count in ((dy, gy, ny), (dx, gx, nx)):
            if move == 0:
                continue
            here = pos < count - 1 if move > 0 else pos > 0
            found = here if found is None else jnp.logical_and(found, here)
        return found

    def roll(x, shift):
        shift = shift % lanes
        return pltpu.roll(x, shift, 1) if shift else x

    def make_packs(src, it):
        group = lane_of(rows) // 16
        right = jnp.zeros((rows, lanes), jnp.float32)
        left = right
        for z in range(depth):
            right = jnp.where(group == z, roll(src[z, :, cols - lanes : cols], 16 * z + 9), right)
            left = jnp.where(group == z, roll(src[z, :, 0:lanes], 16 * z), left)
            row_out[it, 0, z : z + 1] = src[z, rows - 9 : rows - 8, :]
            row_out[it, 1, z : z + 1] = src[z, 8:9, :]
        pack_out[it, 0] = right
        pack_out[it, 1] = left

    def copies(src, it, d):
        dy, dx = DIRS[d]
        pairs = []
        if dx == 0:
            start = rows - 8 if dy > 0 else 0
            pairs.append((src.at[:, start : start + 8, :], rows_in.at[it, d]))
            pairs.append((row_out.at[it, d], row_in.at[it, d]))
            start = rows - 16 if dy > 0 else 0
            pairs.append((pack_out.at[it, :, start : start + 16], side_in.at[it, d]))
        elif dy == 0:
            pairs.append((pack_out.at[it, d - 2], pack_in.at[it, d - 2]))
        else:
            start = rows - 16 if dy > 0 else 0
            pairs.append((pack_out.at[it, 0 if dx > 0 else 1, start : start + 16], corner_in.at[it, d - 4]))
        if it == 0:
            at = {1: slice(cols - lanes, cols), -1: slice(0, lanes), 0: slice(0, cols)}[dx]
            pairs.append((own_tiss.at[:, at], near_tiss.at[d, :, at]))
        return [
            pltpu.make_async_remote_copy(
                src_ref=a,
                dst_ref=b,
                send_sem=halo_send.at[it, d, j],
                recv_sem=halo_recv.at[it, d, j],
                device_id={"gy": gy + dy, "gx": gx + dx},
                device_id_type=MESH,
            )
            for j, (a, b) in enumerate(pairs)
        ]

    def clear_missing(it):
        for d, (dy, dx) in enumerate(DIRS):

            @pl.when(jnp.logical_not(exists(-dy, -dx)))
            def _():
                if dx == 0:
                    rows_in[it, d] = jnp.zeros(rows_in.shape[2:], jnp.float32)
                    row_in[it, d] = jnp.zeros(row_in.shape[2:], jnp.float32)
                    side_in[it, d] = jnp.zeros(side_in.shape[2:], jnp.float32)
                elif dy == 0:
                    pack_in[it, d - 2] = jnp.zeros(pack_in.shape[2:], jnp.float32)
                else:
                    corner_in[it, d - 4] = jnp.zeros(corner_in.shape[2:], jnp.float32)
                if it == 0:
                    near_tiss[d] = jnp.zeros(near_tiss.shape[1:], jnp.float32)

    def start_halo(src, it):
        for d, (dy, dx) in enumerate(DIRS):

            @pl.when(exists(dy, dx))
            def _():
                for copy in copies(src, it, d):
                    copy.start()

    def wait_halo(src, it):
        for d, (dy, dx) in enumerate(DIRS):

            @pl.when(exists(-dy, -dx))
            def _():
                for copy in copies(src, it, d):
                    copy.wait_recv()

    def wait_sent(src, it):
        for d, (dy, dx) in enumerate(DIRS):

            @pl.when(exists(dy, dx))
            def _():
                for copy in copies(src, it, d):
                    copy.wait_send()

    def sum_copy(k):
        flat = lax.rem(me + k, peers)
        return pltpu.make_async_remote_copy(
            src_ref=sums.at[0],
            dst_ref=sums.at[k],
            send_sem=sum_send.at[k],
            recv_sem=sum_recv.at[k],
            device_id={"gy": flat // nx, "gx": lax.rem(flat, nx)},
            device_id_type=MESH,
        )

    def spread(ref, index, flags):
        for k in range(nb + 2):
            ref[index + (slice(8 * k, 8 * k + 8),)] = jnp.broadcast_to(flags[k : k + 1], (8, lanes))

    def spread_tissue():
        lane = lane_of(8)
        spot = lane % 16
        inner = jnp.logical_and(lane > 0, lane < lanes - 1)
        valid = jnp.logical_or(
            jnp.logical_and(spot >= 1, spot <= 9), jnp.logical_and(spot >= 12, spot <= 14)
        )
        patterns = {}
        for zb in range(blocks_z):
            first = zb * blocks_y
            wide_tiss[zb, 1 : 1 + blocks_y, lanes : lanes + cols] = own_tiss[first : first + blocks_y]
            wide_tiss[zb, 1 : 1 + blocks_y, 0:lanes] = near_tiss[2, first : first + blocks_y, cols - lanes : cols]
            wide_tiss[zb, 1 : 1 + blocks_y, lanes + cols :] = near_tiss[3, first : first + blocks_y, 0:lanes]
            for row, source, at in ((0, (0, 4, 5), first + blocks_y - 1), (1 + blocks_y, (1, 6, 7), first)):
                mid_d, left_d, right_d = source
                wide_tiss[zb, row : row + 1, lanes : lanes + cols] = near_tiss[mid_d, at : at + 1, :]
                wide_tiss[zb, row : row + 1, 0:lanes] = near_tiss[left_d, at : at + 1, cols - lanes : cols]
                wide_tiss[zb, row : row + 1, lanes + cols :] = near_tiss[right_d, at : at + 1, 0:lanes]
            for ci in range(2):
                c = 8 * ci
                for t in range(2):
                    off = lanes + step * t + c
                    flags = (wide_tiss[zb, 0:8, off : off + lanes] - 1.0) * BIG
                    if ci == 0:
                        flags = jnp.where(inner, flags, -BIG)
                    spread(pens, (ci, t, zb), flags)
                left = wide_tiss[zb, 0:8, lanes - 9 + c : 2 * lanes - 9 + c]
                off = lanes + 2 * step + c - 11
                right = wide_tiss[zb, 0:8, off : off + lanes]
                part = jnp.where(lane < 11, left, jnp.where(lane < 16, right, 0.0))
                for shift in (16, 32, 64):
                    part = part + roll(part, shift)
                patterns[zb, ci] = (part - 1.0) * BIG
        low = lane < lanes // 2
        both = [jnp.where(low, patterns[0, ci], patterns[1, ci]) for ci in range(2)]
        own = jnp.where(valid, both[0], -BIG)
        spread(ppens, (0,), own)
        spread(ppens, (1,), both[1])
        spread(ppens, (2,), jnp.where(low, own, -BIG))
        spread(ppens, (3,), patterns[1, 0])
        spread(ppens, (4,), patterns[1, 1])
        spread(ppens, (5,), jnp.where(low, -BIG, own))
        spread(ppens, (6,), patterns[0, 1])

    def shifted(n0, n1, extra):
        lane = lane_of(n0.shape[0])
        return (
            n0,
            jnp.where(lane < 2, roll(n0, 2), roll(n1, 2)),
            jnp.where(lane < lanes - 8, roll(n0, -8), roll(n1, -8)),
            roll(n1, -6) if extra is None else jnp.where(lane < lanes - 6, roll(n1, -6), extra),
        )

    def fill_own(src):
        for z in range(depth):
            four = shifted(src[z, :, 0:lanes], src[z, :, lanes : 2 * lanes], None)
            for k, part in enumerate(four):
                vals[k // 2, k % 2, z, PAD : PAD + rows] = part

    def fill_halo(it):
        lane = lane_of(rows)
        for z in range(depth):
            extra = roll(pack_in[it, 1], lanes - 6 - 16 * z)
            vals[1, 1, z, PAD : PAD + rows] = jnp.where(
                lane < lanes - 6, vals[1, 1, z, PAD : PAD + rows], extra
            )
        plane = lax.broadcasted_iota(jnp.int32, (depth, lanes), 0)
        for d, corner, at, single, alone in (
            (0, 1, 8, 7, PAD - 9), (1, 3, 0, 8, PAD + rows + 8)
        ):
            start = PAD - 8 if d == 0 else PAD + rows
            for z in range(depth):
                extra = roll(corner_in[it, corner, at : at + 8], lanes - 6 - 16 * z)
                four = shifted(rows_in[it, d, z, :, 0:lanes], rows_in[it, d, z, :, lanes : 2 * lanes], extra)
                for k, part in enumerate(four):
                    vals[k // 2, k % 2, z, start : start + 8] = part
            line = jnp.broadcast_to(corner_in[it, corner, single : single + 1], (depth, lanes))
            extra = jnp.zeros((depth, lanes), jnp.float32)
            for z in range(depth):
                extra = jnp.where(plane == z, roll(line, lanes - 6 - 16 * z), extra)
            four = shifted(row_in[it, d, :, 0:lanes], row_in[it, d, :, lanes : 2 * lanes], extra)
            for k, part in enumerate(four):
                for z in range(depth):
                    vals[k // 2, k % 2, z, alone : alone + 1] = part[z : z + 1]
        for start, right_of_left, left, right, left_of_right in (
            (0, corner_in[it, 0], side_in[it, 0, 1], side_in[it, 0, 0], corner_in[it, 1]),
            (PAD, pack_in[it, 0], pack_out[it, 1], pack_out[it, 0], pack_in[it, 1]),
            (PAD + rows, corner_in[it, 2], side_in[it, 1, 1], side_in[it, 1, 0], corner_in[it, 3]),
        ):
            size = left.shape[0]
            lane = lane_of(size)
            spot, group = lane % 16, lane // 16
            zero = jnp.where(
                spot < 9,
                right_of_left,
                jnp.where(
                    spot < 11, roll(left, 9), jnp.where(spot < 15, roll(right, 6), roll(left_of_right, 15))
                ),
            )
            eight = jnp.where(
                spot < 1, roll(right_of_left, -8), jnp.where(spot < 11, roll(left, 1), roll(left_of_right, 7))
            )
            hole = jnp.logical_and(group >= 4, group < 7)
            at = slice(start, start + size)
            packs[0, at] = zero
            packs[1, at] = eight
            packs[2, at] = jnp.where(group == 7, 0.0, zero)
            packs[3, at] = jnp.where(hole, 0.0, roll(zero, 64))
            packs[4, at] = jnp.where(hole, 0.0, roll(eight, 64))
            gap = jnp.logical_and(group >= 1, group < 4)
            packs[5, at] = jnp.where(group == 0, 0.0, zero)
            packs[6, at] = jnp.where(gap, 0.0, roll(eight, 64))
        for t in range(2):
            for ci in range(2):
                for k in range(2):
                    plane = vals[ci, t, depth // 2 - 1 + k]
                    squares[k, ci, t] = plane * plane

    def extent(b):
        k0 = -1 if b > 0 else 0
        k1 = nb + 1 if b < 0 else nb
        return k0, k1, PAD + 8 * (k0 - 1), 8 * (k1 - k0 + 2)

    def add(ref, index, value, init):
        ref[index] = value if init else ref[index] + value

    def weigh(slot, cube, penalty, differ, scale):
        size = cube.shape[0]
        cubes[slot, 0:size] = cube
        inner = size - 16
        total = cube[8 : 8 + inner] + cubes[slot, 7 : 7 + inner] + cubes[slot, 9 : 9 + inner]
        total = total + roll(total, 1) + roll(total, -1)
        weight = jnp.exp2(penalty - total * scale[0:inner])
        return weight, weight * differ[8 : 8 + inner]

    def main_offset(t, offset, init, scale, slot):
        a, b, c = offset
        ci, bb = c // 8, b // 8
        k0, k1, lo, size = extent(b)
        low, planes = max(0, -a), depth - abs(a)
        own_at, far_at = slice(lo, lo + size), slice(lo + b, lo + b + size)

        def differ(z):
            return vals[ci, t, z + a, far_at] - vals[0, t, z, own_at]

        def outside(z):
            if a == 0:
                return None
            if (z < low) == (a > 0):
                return squares[0 if a > 0 else 1, ci, t, far_at]
            return squares[1 if a > 0 else 0, 0, t, own_at]

        own_pen, far_pen = slice(8 * (k0 + 1), 8 * (k1 + 1)), slice(8 * (k0 + bb + 1), 8 * (k1 + bb + 1))
        po, qo = -8 * k0, -8 * (bb + k0)
        penalty = None
        high = low + planes
        before = outside(low - 1)
        diffs = {low: differ(low)}
        sqs = {low: diffs[low] * diffs[low]}
        for z in range(low, high, 2):
            zb = z // 4
            if z % 4 == 0:
                penalty = pens[0, t, zb, own_pen] + pens[ci, t, (z + a) // 4, far_pen]
            diffs[z + 1] = differ(z + 1)
            sqs[z + 1] = diffs[z + 1] * diffs[z + 1]
            pair = sqs[z] + sqs[z + 1]
            if z + 2 < high:
                diffs[z + 2] = differ(z + 2)
                sqs[z + 2] = diffs[z + 2] * diffs[z + 2]
                after = sqs[z + 2]
            else:
                after = outside(high)
            for plane, cube in (
                (z, pair if before is None else pair + before),
                (z + 1, pair if after is None else pair + after),
            ):
                weight, push = weigh(slot % SLOTS, cube, penalty, diffs[plane], scale)
                slot += 1
                add(acc, (0, 0, t, plane), push[po : po + rows], init)
                add(acc, (0, 1, t, plane), weight[po : po + rows], init)
                far = plane + a
                add(acc, (ci, 0, t, far), -push[qo : qo + rows] if init else -push[qo : qo + rows], init)
                add(acc, (ci, 1, t, far), weight[qo : qo + rows], init)
            before = sqs[z + 1]
        return slot

    def pack_offset(offset, init, scale, slot):
        a, b, c = offset
        ci, bb = c // 8, b // 8
        k0, k1, lo, size = extent(b)
        near, far = {0: (0, ci), 4: (2, 3 + ci), -4: (5, 6)}[a]
        differ = packs[far, lo + b : lo + b + size] - packs[near, lo : lo + size]
        square = differ * differ
        up, down = roll(square, 16), roll(square, -16)
        if a == 0:
            lane = lane_of(size)
            up = jnp.where(lane >= 16, up, 0.0)
            down = jnp.where(lane < lanes - 16, down, 0.0)
        penalty = ppens[near, 8 * (k0 + 1) : 8 * (k1 + 1)] + ppens[far, 8 * (k0 + bb + 1) : 8 * (k1 + bb + 1)]
        weight, push = weigh(slot, square + up + down, penalty, differ, scale)
        po, qo = -8 * k0, -8 * (bb + k0)
        key = ci + 2 * (a != 0)
        first_p, first_q = init
        add(pacc, (0, 0), push[po : po + rows], first_p)
        add(pacc, (0, 1), weight[po : po + rows], first_p)
        add(pacc, (key, 0), -push[qo : qo + rows], first_q)
        add(pacc, (key, 1), weight[qo : qo + rows], first_q)

    def gather(scale):
        def body(t, carry):
            slot = 0
            for k, offset in enumerate(LEVEL + CROSS):
                slot = main_offset(t, offset, k == 0, scale, slot)
            return carry

        lax.fori_loop(0, 2, body, 0)
        seen = set()
        for k, offset in enumerate(LEVEL + CROSS):
            key = (offset[0] != 0, offset[2])
            fresh = key not in seen and key != (False, 0)
            seen.add(key)
            pack_offset(offset, (k == 0, fresh), scale, k % SLOTS)

    def finish(src, dst):
        lane = lane_of(rows)
        spot = lane % 16
        merged = []
        for kind in range(2):
            zero = pacc[0, kind] + roll(pacc[2, kind], 64)
            eight = pacc[1, kind] + roll(pacc[3, kind], 64)
            eight = eight + jnp.where(spot == 1, roll(zero, -8), 0.0)
            merged.append(
                jnp.where(jnp.logical_or(spot >= 14, spot == 0), roll(zero, -14), jnp.where(spot < 10, eight, 0.0))
            )
        for z in range(depth):
            sides = []
            for kind in range(2):
                near = roll(merged[kind], -(16 * z + 1))
                first = acc[0, kind, 0, z]
                second = roll(acc[0, kind, 1, z], -2)
                far_first = roll(acc[1, kind, 0, z], 8)
                far_second = roll(acc[1, kind, 1, z], 6)
                sides.append((
                    first + jnp.where(lane < 9, near, far_first) + jnp.where(lane == lanes - 1, second, 0.0),
                    jnp.where(lane >= lanes - 3, near, second) + jnp.where(lane < 7, far_first, far_second),
                ))
            for t in range(2):
                at = slice(t * lanes, (t + 1) * lanes)
                dst[z, :, at] = src[z, :, at] + sides[0][t] / (sides[1][t] + 1.0)

    loads[0].wait()
    widen = (
        lax.broadcasted_iota(jnp.int32, (blocks_x, cols), 1) // 8
        == lax.broadcasted_iota(jnp.int32, (blocks_x, cols), 0)
    ).astype(jnp.float32)
    for zb in range(blocks_z):
        flags = mask_ref[zb].astype(jnp.float32)
        own_tiss[zb * blocks_y : (zb + 1) * blocks_y] = jnp.dot(
            flags, widen, preferred_element_type=jnp.float32
        )
    loads[1].wait()
    total = jnp.zeros((8, cols), jnp.float32)
    count = jnp.zeros((8, cols), jnp.float32)
    for z in range(1, depth - 1):
        residual = vol_ref[z] - 0.5 * (vol_ref[z - 1] + vol_ref[z + 1])
        for yb in range(blocks_y):
            line = (z // 4) * blocks_y + yb
            flag = jnp.broadcast_to(own_tiss[line : line + 1], (8, cols))
            piece = residual[8 * yb : 8 * yb + 8]
            total = total + flag * piece * piece
            count = count + flag
    total = jnp.sum(total, axis=0, keepdims=True)
    count = jnp.sum(count, axis=0, keepdims=True)
    tiles = cols // lanes
    total = functools.reduce(jnp.add, [total[:, i * lanes : (i + 1) * lanes] for i in range(tiles)])
    count = functools.reduce(jnp.add, [count[:, i * lanes : (i + 1) * lanes] for i in range(tiles)])
    lane = lax.broadcasted_iota(jnp.int32, (1, lanes), 1)
    sums[0] = jnp.where(
        lane < lanes // 2,
        jnp.sum(total, axis=1, keepdims=True),
        jnp.sum(count, axis=1, keepdims=True),
    )
    make_packs(vol_ref, 0)
    pl.semaphore_wait(barrier, peers - 1)
    for k in range(1, peers):
        sum_copy(k).start()
    start_halo(vol_ref, 0)
    for it in range(ITERS):
        clear_missing(it)
    fill_own(vol_ref)
    wait_halo(vol_ref, 0)
    spread_tissue()
    fill_halo(0)
    for k in range(1, peers):
        sum_copy(k).wait_recv()
    everything = sums[0]
    for k in range(1, peers):
        everything = everything + sums[k]
    summed = everything[:, 0:1] * (2.0 / 3.0)
    tissue_count = everything[:, lanes // 2 : lanes // 2 + 1]
    variance = summed / jnp.maximum(tissue_count, 1.0) + 1e-05
    width = 54.0 * smooth_ref[0] * smooth_ref[0]
    scale = jnp.broadcast_to(LOG2E / (width * variance), (rows + 8, lanes))
    gather(scale)
    finish(vol_ref, mid)
    make_packs(mid, 1)
    start_halo(mid, 1)
    fill_own(mid)
    wait_halo(mid, 1)
    fill_halo(1)
    gather(scale)
    finish(mid, out_ref)
    wait_sent(vol_ref, 0)
    wait_sent(mid, 1)
    for k in range(1, peers):
        sum_copy(k).wait_send()


def on_device(volume, tissue_mask, smoothing):
    ny, nx = lax.axis_size("gy"), lax.axis_size("gx")
    depth, rows, cols = volume.shape
    blocks_z, blocks_y, blocks_x = tissue_mask.shape
    lanes = 128
    assert depth == 8 and cols == 2 * lanes and blocks_z == 2
    flag_rows = -(-(blocks_y + 2) // 8) * 8
    f32 = jnp.float32
    vmem = pl.BlockSpec(memory_space=pltpu.VMEM)
    anywhere = pl.BlockSpec(memory_space=pltpu.HBM)
    return pl.pallas_call(
        functools.partial(kernel, ny, nx),
        out_shape=jax.ShapeDtypeStruct(volume.shape, f32),
        in_specs=[pl.BlockSpec(memory_space=pltpu.SMEM), anywhere, anywhere],
        out_specs=vmem,
        scratch_shapes=[
            pltpu.VMEM((depth, rows, cols), f32),
            pltpu.VMEM((blocks_z, blocks_y, blocks_x), jnp.int32),
            pltpu.VMEM((depth, rows, cols), f32),
            pltpu.VMEM((2, 2, depth, rows + 2 * PAD, lanes), f32),
            pltpu.VMEM((7, rows + 2 * PAD, lanes), f32),
            pltpu.VMEM((2, 2, 2, rows + 2 * PAD, lanes), f32),
            pltpu.VMEM((SLOTS, rows + 24, lanes), f32),
            pltpu.VMEM((2, 2, 2, depth, rows, lanes), f32),
            pltpu.VMEM((4, 2, rows, lanes), f32),
            pltpu.VMEM((2, 2, blocks_z, rows + 16, lanes), f32),
            pltpu.VMEM((7, rows + 16, lanes), f32),
            pltpu.VMEM((blocks_z * blocks_y, cols), f32),
            pltpu.VMEM((len(DIRS), blocks_z * blocks_y, cols), f32),
            pltpu.VMEM((blocks_z, flag_rows, cols + 2 * lanes), f32),
            pltpu.VMEM((ITERS, 2, depth, 8, cols), f32),
            pltpu.VMEM((ITERS, 2, depth, cols), f32),
            pltpu.VMEM((ITERS, 2, depth, cols), f32),
            pltpu.VMEM((ITERS, 2, rows, lanes), f32),
            pltpu.VMEM((ITERS, 2, rows, lanes), f32),
            pltpu.VMEM((ITERS, 2, 2, 16, lanes), f32),
            pltpu.VMEM((ITERS, 4, 16, lanes), f32),
            pltpu.VMEM((ny * nx, 1, lanes), f32),
            pltpu.SemaphoreType.DMA((2,)),
            pltpu.SemaphoreType.DMA((ny * nx,)),
            pltpu.SemaphoreType.DMA((ny * nx,)),
            pltpu.SemaphoreType.DMA((ITERS, len(DIRS), 4)),
            pltpu.SemaphoreType.DMA((ITERS, len(DIRS), 4)),
        ],
        compiler_params=pltpu.CompilerParams(
            collective_id=0, has_side_effects=True, vmem_limit_bytes=16 * 2**20
        ),
    )(
        smoothing,
        pltpu.with_memory_space_constraint(volume, pltpu.HBM),
        pltpu.with_memory_space_constraint(tissue_mask, pltpu.HBM),
    )


def solution(mesh):
    placed = (P(None, ("slab", "gy"), "gx"), P(None, ("slab", "gy"), "gx"), P())
    return jax.shard_map(
        on_device,
        mesh=mesh,
        in_specs=placed,
        out_specs=P(None, ("slab", "gy"), "gx"),
        check_vma=False,
    )
```

```python
import functools

import jax
import jax.numpy as jnp
from jax import lax
from jax.experimental import pallas as pl
from jax.experimental.pallas import tpu as pltpu
from jax.sharding import PartitionSpec as P

MESH = pl.DeviceIdType.MESH
ITERS = 2
LOG2E = 1.4426950408889634
BIG = 1e30
DIRS = ((1, 0), (-1, 0), (0, 1), (0, -1), (1, 1), (1, -1), (-1, 1), (-1, -1))
LEVEL = ((0, 0, 8), (0, 8, 8), (0, -8, 8), (0, 8, 0))
CROSS = (
    (4, 0, 8), (4, 8, 8), (4, -8, 8), (-4, 0, 8), (-4, 8, 8), (-4, -8, 8), (4, 0, 0), (4, 8, 0), (4, -8, 0)
)
PAD = 16
SLOTS = 32


def kernel(
    ny, nx, smooth_ref, vol_hbm, mask_hbm, out_ref, vol_ref, mask_ref, mid, vals, packs, squares,
    cubes, totals, band, acc, pcubes, found, pens, ppens, own_tiss, near_tiss, wide_tiss,
    rows_in, row_in, row_out, pack_out, pack_in, corner_in, row_sums, col_sums,
    load_sem, known, sum_send, sum_recv, halo_send, halo_recv,
):
    depth, rows, cols = vol_ref.shape
    lanes = 128
    blocks_z, blocks_y, blocks_x = mask_ref.shape
    nb = rows // 8
    step = lanes - 2
    gy, gx = lax.axis_index("gy"), lax.axis_index("gx")

    barrier = pltpu.get_barrier_semaphore()

    def exists(dy, dx):
        found = None
        for move, pos, count in ((dy, gy, ny), (dx, gx, nx)):
            if move == 0:
                continue
            here = pos < count - move if move > 0 else pos >= -move
            found = here if found is None else jnp.logical_and(found, here)
        return found

    def peer(axis, k):
        pos, count = (gy, ny) if axis == "gy" else (gx, nx)
        return {axis: jnp.where(pos + k >= count, pos + k - count, pos + k)}

    def greet(semaphore, moves):
        for dy, dx in moves:

            @pl.when(exists(dy, dx))
            def _():
                pl.semaphore_signal(
                    semaphore, inc=1, device_id={"gy": gy + dy, "gx": gx + dx}, device_id_type=MESH
                )

    def present(moves):
        return functools.reduce(jnp.add, [exists(dy, dx).astype(jnp.int32) for dy, dx in moves])

    column = [(dy, 0) for dy in (1, -1, 2, -2)]
    others = column + list(DIRS[4:])
    for k in range(1, nx):
        pl.semaphore_signal(barrier, inc=1, device_id=peer("gx", k), device_id_type=MESH)
    greet(barrier, others)

    loads = [
        pltpu.make_async_copy(mask_hbm, mask_ref, load_sem.at[0]),
        pltpu.make_async_copy(vol_hbm, vol_ref, load_sem.at[1]),
    ]
    for load in loads:
        load.start()

    def lane_of(n):
        return lax.broadcasted_iota(jnp.int32, (n, lanes), 1)

    def roll(x, shift):
        shift = shift % lanes
        return pltpu.roll(x, shift, 1) if shift else x

    def packed(planes):
        group = lane_of(planes[0].shape[0]) // 16
        left, right = planes[0][:, 0:lanes], roll(planes[0][:, cols - lanes : cols], 9)
        for z in range(1, depth):
            right = jnp.where(group == z, roll(planes[z][:, cols - lanes : cols], 16 * z + 9), right)
            left = jnp.where(group == z, roll(planes[z][:, 0:lanes], 16 * z), left)
        return left, right

    def make_packs(src, it):
        for z in range(depth):
            row_out[it, 0, z : z + 1] = src[z, rows - 9 : rows - 8, :]
            row_out[it, 1, z : z + 1] = src[z, 8:9, :]
        left, right = packed([src[z] for z in range(depth)])
        pack_out[it, 0] = right
        pack_out[it, 1] = left

    def copies(src, it, d):
        dy, dx = DIRS[d]
        pairs = []
        if dx == 0:
            start = rows - 8 if dy > 0 else 0
            pairs.append((src.at[:, start : start + 8, :], rows_in.at[it, d]))
            pairs.append((row_out.at[it, d], row_in.at[it, d]))
        elif dy == 0:
            pairs.append((pack_out.at[it, d - 2], pack_in.at[it, d - 2]))
        else:
            start = rows - 16 if dy > 0 else 0
            pairs.append((pack_out.at[it, 0 if dx > 0 else 1, start : start + 16], corner_in.at[it, d - 4]))
        if it == 0:
            at = {1: slice(cols - lanes, cols), -1: slice(0, lanes), 0: slice(0, cols)}[dx]
            pairs.append((own_tiss.at[:, at], near_tiss.at[d, :, at]))
        return [
            pltpu.make_async_remote_copy(
                src_ref=a,
                dst_ref=b,
                send_sem=halo_send.at[it, d, j],
                recv_sem=halo_recv.at[it, d, j],
                device_id={"gy": gy + dy, "gx": gx + dx},
                device_id_type=MESH,
            )
            for j, (a, b) in enumerate(pairs)
        ]

    def clear_missing(it):
        for d, (dy, dx) in enumerate(DIRS):

            @pl.when(jnp.logical_not(exists(-dy, -dx)))
            def _():
                if dx == 0:
                    rows_in[it, d] = jnp.zeros(rows_in.shape[2:], jnp.float32)
                    row_in[it, d] = jnp.zeros(row_in.shape[2:], jnp.float32)
                elif dy == 0:
                    pack_in[it, d - 2] = jnp.zeros(pack_in.shape[2:], jnp.float32)
                else:
                    corner_in[it, d - 4] = jnp.zeros(corner_in.shape[2:], jnp.float32)
                if it == 0:
                    near_tiss[d] = jnp.zeros(near_tiss.shape[1:], jnp.float32)

    def start_halo(src, it):
        for d, (dy, dx) in enumerate(DIRS):

            @pl.when(exists(dy, dx))
            def _():
                for copy in copies(src, it, d):
                    copy.start()

    def wait_halo(src, it):
        for d, (dy, dx) in enumerate(DIRS):

            @pl.when(exists(-dy, -dx))
            def _():
                for copy in copies(src, it, d):
                    copy.wait_recv()

    def wait_sent(src, it):
        for d, (dy, dx) in enumerate(DIRS):

            @pl.when(exists(dy, dx))
            def _():
                for copy in copies(src, it, d):
                    copy.wait_send()

    def sum_copies(axis):
        count, buffer = (nx, row_sums) if axis == "gx" else (ny, col_sums)
        stage = 0 if axis == "gx" else 1
        return [
            pltpu.make_async_remote_copy(
                src_ref=buffer.at[0],
                dst_ref=buffer.at[k],
                send_sem=sum_send.at[stage, k],
                recv_sem=sum_recv.at[stage, k],
                device_id=peer(axis, k),
                device_id_type=MESH,
            )
            for k in range(1, count)
        ]

    def spread(ref, index, flags):
        for k in range(nb + 2):
            ref[index + (slice(8 * k, 8 * k + 8),)] = jnp.broadcast_to(flags[k : k + 1], (8, lanes))

    def spread_tissue():
        lane = lane_of(8)
        spot = lane % 16
        inner = jnp.logical_and(lane > 0, lane < lanes - 1)
        valid = jnp.logical_or(
            jnp.logical_and(spot >= 1, spot <= 9), jnp.logical_and(spot >= 12, spot <= 14)
        )
        patterns = {}
        for zb in range(blocks_z):
            first = zb * blocks_y
            wide_tiss[zb, 1 : 1 + blocks_y, lanes : lanes + cols] = own_tiss[first : first + blocks_y]
            wide_tiss[zb, 1 : 1 + blocks_y, 0:lanes] = near_tiss[2, first : first + blocks_y, cols - lanes : cols]
            wide_tiss[zb, 1 : 1 + blocks_y, lanes + cols :] = near_tiss[3, first : first + blocks_y, 0:lanes]
            for row, source, at in ((0, (0, 4, 5), first + blocks_y - 1), (1 + blocks_y, (1, 6, 7), first)):
                mid_d, left_d, right_d = source
                wide_tiss[zb, row : row + 1, lanes : lanes + cols] = near_tiss[mid_d, at : at + 1, :]
                wide_tiss[zb, row : row + 1, 0:lanes] = near_tiss[left_d, at : at + 1, cols - lanes : cols]
                wide_tiss[zb, row : row + 1, lanes + cols :] = near_tiss[right_d, at : at + 1, 0:lanes]
            for ci in range(2):
                c = 8 * ci
                for t in range(2):
                    off = lanes + step * t + c
                    flags = (wide_tiss[zb, 0:8, off : off + lanes] - 1.0) * BIG
                    if ci == 0:
                        flags = jnp.where(inner, flags, -BIG)
                    spread(pens, (ci, t, zb), flags)
                left = wide_tiss[zb, 0:8, lanes - 9 + c : 2 * lanes - 9 + c]
                off = lanes + 2 * step + c - 11
                right = wide_tiss[zb, 0:8, off : off + lanes]
                part = jnp.where(lane < 11, left, jnp.where(lane < 16, right, 0.0))
                for shift in (16, 32, 64):
                    part = part + roll(part, shift)
                patterns[zb, ci] = (part - 1.0) * BIG
        low = lane < lanes // 2
        both = [jnp.where(low, patterns[0, ci], patterns[1, ci]) for ci in range(2)]
        own = jnp.where(valid, both[0], -BIG)
        spread(ppens, (0,), own)
        spread(ppens, (1,), both[1])
        spread(ppens, (2,), jnp.where(low, own, -BIG))
        spread(ppens, (3,), patterns[1, 0])
        spread(ppens, (4,), patterns[1, 1])
        spread(ppens, (5,), jnp.where(low, -BIG, own))
        spread(ppens, (6,), patterns[0, 1])
        spread(ppens, (7,), patterns[0, 0])

    def shifted(n0, n1, extra):
        lane = lane_of(n0.shape[0])
        return (
            n0,
            jnp.where(lane < 2, roll(n0, 2), roll(n1, 2)),
            jnp.where(lane < lanes - 8, roll(n0, -8), roll(n1, -8)),
            roll(n1, -6) if extra is None else jnp.where(lane < lanes - 6, roll(n1, -6), extra),
        )

    def fill_own(src):
        for z in range(depth):
            four = shifted(src[z, :, 0:lanes], src[z, :, lanes : 2 * lanes], None)
            for k, part in enumerate(four):
                vals[k // 2, k % 2, z, PAD : PAD + rows] = part

    def fill_halo(it):
        lane = lane_of(rows)
        for z in range(depth):
            extra = roll(pack_in[it, 1], lanes - 6 - 16 * z)
            vals[1, 1, z, PAD : PAD + rows] = jnp.where(
                lane < lanes - 6, vals[1, 1, z, PAD : PAD + rows], extra
            )
        plane = lax.broadcasted_iota(jnp.int32, (depth, lanes), 0)
        for d, corner, at, single, alone in (
            (0, 1, 8, 7, PAD - 9), (1, 3, 0, 8, PAD + rows + 8)
        ):
            start = PAD - 8 if d == 0 else PAD + rows
            for z in range(depth):
                extra = roll(corner_in[it, corner, at : at + 8], lanes - 6 - 16 * z)
                four = shifted(rows_in[it, d, z, :, 0:lanes], rows_in[it, d, z, :, lanes : 2 * lanes], extra)
                for k, part in enumerate(four):
                    vals[k // 2, k % 2, z, start : start + 8] = part
            line = jnp.broadcast_to(corner_in[it, corner, single : single + 1], (depth, lanes))
            extra = jnp.zeros((depth, lanes), jnp.float32)
            for z in range(depth):
                extra = jnp.where(plane == z, roll(line, lanes - 6 - 16 * z), extra)
            four = shifted(row_in[it, d, :, 0:lanes], row_in[it, d, :, lanes : 2 * lanes], extra)
            for k, part in enumerate(four):
                for z in range(depth):
                    vals[k // 2, k % 2, z, alone : alone + 1] = part[z : z + 1]
        parts = [(PAD, pack_in[it, 0], (pack_out[it, 1], pack_out[it, 0]), pack_in[it, 1])]
        for d, at, single in ((0, 8, 7), (1, 0, 8)):
            before, after = corner_in[it, 2 * d], corner_in[it, 2 * d + 1]
            start = PAD - 8 if d == 0 else PAD + rows
            alone = PAD - 9 if d == 0 else PAD + rows + 8
            near = packed([rows_in[it, d, z] for z in range(depth)])
            line = packed([row_in[it, d, z : z + 1] for z in range(depth)])
            parts.append((start, before[at : at + 8], near, after[at : at + 8]))
            parts.append((alone, before[single : single + 1], line, after[single : single + 1]))
        for start, right_of_left, (left, right), left_of_right in parts:
            size = left.shape[0]
            lane = lane_of(size)
            spot, group = lane % 16, lane // 16
            zero = jnp.where(
                spot < 9,
                right_of_left,
                jnp.where(
                    spot < 11, roll(left, 9), jnp.where(spot < 15, roll(right, 6), roll(left_of_right, 15))
                ),
            )
            eight = jnp.where(
                spot < 1, roll(right_of_left, -8), jnp.where(spot < 11, roll(left, 1), roll(left_of_right, 7))
            )
            hole = jnp.logical_and(group >= 4, group < 7)
            at = slice(start, start + size)
            packs[0, at] = zero
            packs[1, at] = eight
            packs[2, at] = jnp.where(group == 7, 0.0, zero)
            packs[3, at] = jnp.where(hole, 0.0, roll(zero, 64))
            packs[4, at] = jnp.where(hole, 0.0, roll(eight, 64))
            gap = jnp.logical_and(group >= 1, group < 4)
            packs[5, at] = jnp.where(group == 0, 0.0, zero)
            packs[6, at] = jnp.where(gap, 0.0, roll(eight, 64))
            packs[7, at] = jnp.where(gap, 0.0, roll(zero, 64))
        for t in range(2):
            for ci in range(2):
                for k in range(2):
                    plane = vals[ci, t, depth // 2 - 1 + k]
                    squares[k, ci, t] = plane * plane

    def extent(b):
        k0 = -1 if b > 0 else 0
        k1 = nb + 1 if b < 0 else nb
        return k0, k1, PAD + 8 * (k0 - 1), 8 * (k1 - k0 + 2)

    def add(ref, index, value, init):
        ref[index] = value if init else ref[index] + value

    def box(parts):
        tops = [part.astype(jnp.bfloat16).astype(jnp.float32) for part in parts]
        lhs = [jnp.concatenate([top, part - top], axis=1) for part, top in zip(parts, tops)]
        return jnp.dot(jnp.concatenate(lhs, axis=0), band[...], preferred_element_type=jnp.float32)

    def main_offset(t, offset, init, scale, slot, mode):
        a, b, c = offset
        ci, bb = c // 8, b // 8
        k0, k1, lo, size = extent(b)
        inner = size - 16
        low, planes = max(0, -a), depth - abs(a)
        high = low + planes

        def differ(z, low_row, count):
            far = slice(low_row + b, low_row + b + count)
            return vals[ci, t, z + a, far] - vals[0, t, z, low_row : low_row + count]

        def outside(z):
            if a == 0:
                return None
            if (z < low) == (a > 0):
                return squares[0 if a > 0 else 1, ci, t, lo + b : lo + b + size]
            return squares[1 if a > 0 else 0, 0, t, lo : lo + size]

        own_pen, far_pen = slice(8 * (k0 + 1), 8 * (k1 + 1)), slice(8 * (k0 + bb + 1), 8 * (k1 + bb + 1))
        po, qo = -8 * k0, -8 * (bb + k0)
        penalty = None
        before = None
        diffs, sqs = {}, {}
        queue = []

        def grow(z):
            diffs[z] = differ(z, lo, size)
            sqs[z] = diffs[z] * diffs[z]

        if mode != "apply":
            before = outside(low - 1)
            grow(low)
        for z in range(low, high, 2):
            if z % 4 == 0 and mode != "measure":
                penalty = pens[0, t, z // 4, own_pen] + pens[ci, t, (z + a) // 4, far_pen]
            cubed = (None, None)
            if mode != "apply":
                grow(z + 1)
                pair = sqs[z] + sqs[z + 1]
                if z + 2 < high:
                    grow(z + 2)
                    after = sqs[z + 2]
                else:
                    after = outside(high)
                cubed = (
                    pair if before is None else pair + before,
                    pair if after is None else pair + after,
                )
                before = sqs[z + 1]
            for plane, cube in zip((z, z + 1), cubed):
                if mode != "apply":
                    at = slot % SLOTS
                    cubes[at, 0:size] = cube
                    total = cube[8 : 8 + inner] + cubes[at, 7 : 7 + inner] + cubes[at, 9 : 9 + inner]
                    if mode == "measure":
                        slot += 1
                        queue.append(total)
                        continue
                    total = total + roll(total, 1) + roll(total, -1)
                if mode == "apply":
                    total = totals[t, slot, 0:inner]
                    gap = differ(plane, lo + 8, inner)
                else:
                    gap = diffs[plane][8 : 8 + inner]
                slot += 1
                weight = jnp.exp2(penalty - total * scale[0:inner])
                push = weight * gap
                add(acc, (0, 0, t, plane), push[po : po + rows], init)
                add(acc, (0, 1, t, plane), weight[po : po + rows], init)
                far = plane + a
                if init:
                    acc[ci, 0, t, far] = -push[qo : qo + rows]
                else:
                    acc[ci, 0, t, far] -= push[qo : qo + rows]
                add(acc, (ci, 1, t, far), weight[qo : qo + rows], init)
        if mode == "measure":
            summed = box(queue)
            for k in range(len(queue)):
                totals[t, slot - len(queue) + k, 0:inner] = summed[k * inner : (k + 1) * inner]
        return slot

    def main_gather(t, scale, mode):
        slot = 0
        for k, offset in enumerate(LEVEL + CROSS):
            slot = main_offset(t, offset, k == 0, scale, slot, mode)
        return 0

    packed_items = []
    for a, b, c in LEVEL + CROSS:
        near, far = {0: (0, c // 8), 4: (2, 3 + c // 8), -4: (5, 6)}[a]
        packed_items.append((near, far, b, c // 8 + 2 * (a != 0), a == 0))

    def pack_differ(near, far, b, low, size):
        return packs[far, low + b : low + b + size] - packs[near, low : low + size]

    def pack_measure():
        for k, (near, far, b, key, masked) in enumerate(packed_items):
            k0, k1, lo, size = extent(b)
            gap = pack_differ(near, far, b, lo, size)
            square = gap * gap
            up, down = roll(square, 16), roll(square, -16)
            if masked:
                lane = lane_of(size)
                up = jnp.where(lane >= 16, up, 0.0)
                down = jnp.where(lane < lanes - 16, down, 0.0)
            pcubes[k, 0:size] = square + up + down
        for k, (near, far, b, key, masked) in enumerate(packed_items):
            inner = extent(b)[3] - 16
            total = pcubes[k, 7 : 7 + inner] + pcubes[k, 8 : 8 + inner] + pcubes[k, 9 : 9 + inner]
            found[k, 0:inner] = total + roll(total, 1) + roll(total, -1)

    def pack_apply(scale):
        parts = [[None] * 4, [None] * 4]

        def gain(kind, key, value, minus):
            old = parts[kind][key]
            if old is None:
                parts[kind][key] = -value if minus else value
            else:
                parts[kind][key] = old - value if minus else old + value

        for k, (near, far, b, key, masked) in enumerate(packed_items):
            k0, k1, lo, size = extent(b)
            bb, inner = b // 8, size - 16
            penalty = ppens[near, 8 * (k0 + 1) : 8 * (k1 + 1)] + ppens[far, 8 * (k0 + bb + 1) : 8 * (k1 + bb + 1)]
            weight = jnp.exp2(penalty - found[k, 0:inner] * scale[0:inner])
            push = weight * pack_differ(near, far, b, lo + 8, inner)
            po, qo = -8 * k0, -8 * (bb + k0)
            gain(0, 0, push[po : po + rows], False)
            gain(1, 0, weight[po : po + rows], False)
            gain(0, key, push[qo : qo + rows], True)
            gain(1, key, weight[qo : qo + rows], False)
        return parts

    def finish(src, dst, parts):
        lane = lane_of(rows)
        spot = lane % 16
        merged = []
        for kind in range(2):
            zero = parts[kind][0] + roll(parts[kind][2], 64)
            eight = parts[kind][1] + roll(parts[kind][3], 64)
            eight = eight + jnp.where(spot == 1, roll(zero, -8), 0.0)
            merged.append(
                jnp.where(jnp.logical_or(spot >= 14, spot == 0), roll(zero, -14), jnp.where(spot < 10, eight, 0.0))
            )
        for z in range(depth):
            sides = []
            for kind in range(2):
                near = roll(merged[kind], -(16 * z + 1))
                first = acc[0, kind, 0, z]
                second = roll(acc[0, kind, 1, z], -2)
                far_first = roll(acc[1, kind, 0, z], 8)
                far_second = roll(acc[1, kind, 1, z], 6)
                sides.append((
                    first + jnp.where(lane < 9, near, far_first) + jnp.where(lane == lanes - 1, second, 0.0),
                    jnp.where(lane >= lanes - 3, near, second) + jnp.where(lane < 7, far_first, far_second),
                ))
            for t in range(2):
                at = slice(t * lanes, (t + 1) * lanes)
                dst[z, :, at] = src[z, :, at] + sides[0][t] / (sides[1][t] + 1.0)

    row_at = lax.broadcasted_iota(jnp.int32, (2 * lanes, lanes), 0) % lanes
    col_at = lax.broadcasted_iota(jnp.int32, (2 * lanes, lanes), 1)
    band[...] = (jnp.abs(row_at - col_at) <= 1).astype(jnp.float32)
    loads[0].wait()
    widen = (
        lax.broadcasted_iota(jnp.int32, (blocks_x, cols), 1) // 8
        == lax.broadcasted_iota(jnp.int32, (blocks_x, cols), 0)
    ).astype(jnp.float32)
    for zb in range(blocks_z):
        flags = mask_ref[zb].astype(jnp.float32)
        own_tiss[zb * blocks_y : (zb + 1) * blocks_y] = jnp.dot(
            flags, widen, preferred_element_type=jnp.float32
        )
    loads[1].wait()
    total = jnp.zeros((8, cols), jnp.float32)
    count = jnp.zeros((8, cols), jnp.float32)
    for z in range(1, depth - 1):
        residual = vol_ref[z] - 0.5 * (vol_ref[z - 1] + vol_ref[z + 1])
        for yb in range(blocks_y):
            line = (z // 4) * blocks_y + yb
            flag = jnp.broadcast_to(own_tiss[line : line + 1], (8, cols))
            piece = residual[8 * yb : 8 * yb + 8]
            total = total + flag * piece * piece
            count = count + flag
    total = jnp.sum(total, axis=0, keepdims=True)
    count = jnp.sum(count, axis=0, keepdims=True)
    tiles = cols // lanes
    total = functools.reduce(jnp.add, [total[:, i * lanes : (i + 1) * lanes] for i in range(tiles)])
    count = functools.reduce(jnp.add, [count[:, i * lanes : (i + 1) * lanes] for i in range(tiles)])
    lane = lax.broadcasted_iota(jnp.int32, (1, lanes), 1)
    row_sums[0] = jnp.where(
        lane < lanes // 2,
        jnp.sum(total, axis=1, keepdims=True),
        jnp.sum(count, axis=1, keepdims=True),
    )
    make_packs(vol_ref, 0)
    pl.semaphore_wait(barrier, nx - 1 + present(others))
    rounds = known.shape[0]
    for copy in sum_copies("gx"):
        copy.start()
    greet(known.at[0], column)
    start_halo(vol_ref, 0)
    for it in range(ITERS):
        clear_missing(it)
    fill_own(vol_ref)
    for k in range(rounds):
        pl.semaphore_wait(known.at[k], present(column))
        if k + 1 < rounds:
            greet(known.at[k + 1], column)
    for copy in sum_copies("gx"):
        copy.wait_recv()
    col_sums[0] = functools.reduce(jnp.add, [row_sums[k] for k in range(nx)])
    for copy in sum_copies("gy"):
        copy.start()
    wait_halo(vol_ref, 0)
    spread_tissue()
    fill_halo(0)
    lax.fori_loop(0, 2, lambda t, carry: main_gather(t, None, "measure"), 0)
    pack_measure()
    for copy in sum_copies("gy"):
        copy.wait_recv()
    everything = functools.reduce(jnp.add, [col_sums[k] for k in range(ny)])
    summed = everything[:, 0:1] * (2.0 / 3.0)
    tissue_count = everything[:, lanes // 2 : lanes // 2 + 1]
    variance = summed / jnp.maximum(tissue_count, 1.0) + 1e-05
    width = 54.0 * smooth_ref[0] * smooth_ref[0]
    scale = jnp.broadcast_to(LOG2E / (width * variance), (rows + 8, lanes))
    lax.fori_loop(0, 2, lambda t, carry: main_gather(t, scale, "apply"), 0)
    finish(vol_ref, mid, pack_apply(scale))
    make_packs(mid, 1)
    start_halo(mid, 1)
    fill_own(mid)
    wait_halo(mid, 1)
    fill_halo(1)
    lax.fori_loop(0, 2, lambda t, carry: main_gather(t, scale, "both"), 0)
    pack_measure()
    finish(mid, out_ref, pack_apply(scale))
    wait_sent(vol_ref, 0)
    wait_sent(mid, 1)
    for axis in ("gx", "gy"):
        for copy in sum_copies(axis):
            copy.wait_send()


def on_device(volume, tissue_mask, smoothing):
    ny, nx = lax.axis_size("gy"), lax.axis_size("gx")
    depth, rows, cols = volume.shape
    blocks_z, blocks_y, blocks_x = tissue_mask.shape
    lanes = 128
    assert depth == 8 and cols == 2 * lanes and blocks_z == 2
    flag_rows = -(-(blocks_y + 2) // 8) * 8
    f32 = jnp.float32
    vmem = pl.BlockSpec(memory_space=pltpu.VMEM)
    anywhere = pl.BlockSpec(memory_space=pltpu.HBM)
    return pl.pallas_call(
        functools.partial(kernel, ny, nx),
        out_shape=jax.ShapeDtypeStruct(volume.shape, f32),
        in_specs=[pl.BlockSpec(memory_space=pltpu.SMEM), anywhere, anywhere],
        out_specs=vmem,
        scratch_shapes=[
            pltpu.VMEM((depth, rows, cols), f32),
            pltpu.VMEM((blocks_z, blocks_y, blocks_x), jnp.int32),
            pltpu.VMEM((depth, rows, cols), f32),
            pltpu.VMEM((2, 2, depth, rows + 2 * PAD, lanes), f32),
            pltpu.VMEM((8, rows + 2 * PAD, lanes), f32),
            pltpu.VMEM((2, 2, 2, rows + 2 * PAD, lanes), f32),
            pltpu.VMEM((SLOTS, rows + 24, lanes), f32),
            pltpu.VMEM((2, len(LEVEL) * depth + len(CROSS) * depth // 2, rows + 8, lanes), f32),
            pltpu.VMEM((2 * lanes, lanes), f32),
            pltpu.VMEM((2, 2, 2, depth, rows, lanes), f32),
            pltpu.VMEM((13, rows + 24, lanes), f32),
            pltpu.VMEM((13, rows + 8, lanes), f32),
            pltpu.VMEM((2, 2, blocks_z, rows + 16, lanes), f32),
            pltpu.VMEM((8, rows + 16, lanes), f32),
            pltpu.VMEM((blocks_z * blocks_y, cols), f32),
            pltpu.VMEM((len(DIRS), blocks_z * blocks_y, cols), f32),
            pltpu.VMEM((blocks_z, flag_rows, cols + 2 * lanes), f32),
            pltpu.VMEM((ITERS, 2, depth, 8, cols), f32),
            pltpu.VMEM((ITERS, 2, depth, cols), f32),
            pltpu.VMEM((ITERS, 2, depth, cols), f32),
            pltpu.VMEM((ITERS, 2, rows, lanes), f32),
            pltpu.VMEM((ITERS, 2, rows, lanes), f32),
            pltpu.VMEM((ITERS, 4, 16, lanes), f32),
            pltpu.VMEM((nx, 1, lanes), f32),
            pltpu.VMEM((ny, 1, lanes), f32),
            pltpu.SemaphoreType.DMA((2,)),
            pltpu.SemaphoreType.REGULAR((max((ny - 2) // 2, 1),)),
            pltpu.SemaphoreType.DMA((2, max(ny, nx))),
            pltpu.SemaphoreType.DMA((2, max(ny, nx))),
            pltpu.SemaphoreType.DMA((ITERS, len(DIRS), 3)),
            pltpu.SemaphoreType.DMA((ITERS, len(DIRS), 3)),
        ],
        compiler_params=pltpu.CompilerParams(
            collective_id=0, has_side_effects=True, vmem_limit_bytes=16 * 2**20
        ),
    )(
        smoothing,
        pltpu.with_memory_space_constraint(volume, pltpu.HBM),
        pltpu.with_memory_space_constraint(tissue_mask, pltpu.HBM),
    )


def solution(mesh):
    placed = (P(None, ("slab", "gy"), "gx"), P(None, ("slab", "gy"), "gx"), P())
    return jax.shard_map(
        on_device,
        mesh=mesh,
        in_specs=placed,
        out_specs=P(None, ("slab", "gy"), "gx"),
        check_vma=False,
    )
```

```python
import functools

import jax
import jax.numpy as jnp
from jax import lax
from jax.experimental import pallas as pl
from jax.experimental.pallas import tpu as pltpu
from jax.sharding import PartitionSpec as P

MESH = pl.DeviceIdType.MESH
ITERS = 2
LOG2E = 1.4426950408889634
BIG = 1e30
DIRS = ((1, 0), (-1, 0), (0, 1), (0, -1), (1, 1), (1, -1), (-1, 1), (-1, -1))
LEVEL = ((0, 0, 8), (0, 8, 8), (0, -8, 8), (0, 8, 0))
CROSS = (
    (4, 0, 8), (4, 8, 8), (4, -8, 8), (-4, 0, 8), (-4, 8, 8), (-4, -8, 8), (4, 0, 0), (4, 8, 0), (4, -8, 0)
)
PAD = 16
SLOTS = 32


def kernel(
    ny, nx, smooth_ref, vol_hbm, mask_hbm, out_ref, vol_ref, mask_ref, mid, vals, packs, squares,
    cubes, totals, band, acc, pcubes, found, pens, ppens, own_tiss, near_tiss, wide_tiss,
    rows_in, row_in, row_out, pack_out, pack_in, corner_in, row_sums, col_sums,
    load_sem, known, sum_send, sum_recv, halo_send, halo_recv,
):
    depth, rows, cols = vol_ref.shape
    lanes = 128
    blocks_z, blocks_y, blocks_x = mask_ref.shape
    nb = rows // 8
    step = lanes - 2
    gy, gx = lax.axis_index("gy"), lax.axis_index("gx")

    barrier = pltpu.get_barrier_semaphore()

    def exists(dy, dx):
        found = None
        for move, pos, count in ((dy, gy, ny), (dx, gx, nx)):
            if move == 0:
                continue
            here = pos < count - move if move > 0 else pos >= -move
            found = here if found is None else jnp.logical_and(found, here)
        return found

    def peer(axis, k):
        pos, count = (gy, ny) if axis == "gy" else (gx, nx)
        return {axis: jnp.where(pos + k >= count, pos + k - count, pos + k)}

    def greet(semaphore, moves):
        for dy, dx in moves:

            @pl.when(exists(dy, dx))
            def _():
                pl.semaphore_signal(
                    semaphore, inc=1, device_id={"gy": gy + dy, "gx": gx + dx}, device_id_type=MESH
                )

    def present(moves):
        return functools.reduce(jnp.add, [exists(dy, dx).astype(jnp.int32) for dy, dx in moves])

    column = [(dy, 0) for dy in (1, -1, 2, -2)]
    others = column + list(DIRS[4:])
    for k in range(1, nx):
        pl.semaphore_signal(barrier, inc=1, device_id=peer("gx", k), device_id_type=MESH)
    greet(barrier, others)

    loads = [
        pltpu.make_async_copy(mask_hbm, mask_ref, load_sem.at[0]),
        pltpu.make_async_copy(vol_hbm, vol_ref, load_sem.at[1]),
    ]
    for load in loads:
        load.start()

    def lane_of(n):
        return lax.broadcasted_iota(jnp.int32, (n, lanes), 1)

    def roll(x, shift):
        shift = shift % lanes
        return pltpu.roll(x, shift, 1) if shift else x

    def packed(planes):
        group = lane_of(planes[0].shape[0]) // 16
        left, right = planes[0][:, 0:lanes], roll(planes[0][:, cols - lanes : cols], 9)
        for z in range(1, depth):
            right = jnp.where(group == z, roll(planes[z][:, cols - lanes : cols], 16 * z + 9), right)
            left = jnp.where(group == z, roll(planes[z][:, 0:lanes], 16 * z), left)
        return left, right

    def packed_line(line):
        match = lane_of(depth) // 16 == lax.broadcasted_iota(jnp.int32, (depth, lanes), 0)
        ends = []
        for at, shift in ((0, 0), (cols - lanes, 9)):
            moved = pltpu.roll(line[:, at : at + lanes], shift, 1, stride=16, stride_axis=0)
            ends.append(jnp.sum(jnp.where(match, moved, 0.0), axis=0, keepdims=True))
        return ends

    def make_packs(src, it):
        for z in range(depth):
            for d, first, ninth in ((0, rows - 1, rows - 9), (1, 0, 8)):
                row_out[it, d, 0, z : z + 1] = src[z, first : first + 1, :]
                row_out[it, d, 1, z : z + 1] = src[z, ninth : ninth + 1, :]
        left, right = packed([src[z] for z in range(depth)])
        pack_out[it, 0] = right
        pack_out[it, 1] = left

    def copies(src, it, d, late):
        dy, dx = DIRS[d]
        pairs = {}
        if late:
            if dx == 0:
                start = rows - 8 if dy > 0 else 0
                pairs[2] = (src.at[:, start : start + 8, :], rows_in.at[it, d])
                pairs[3] = (row_out.at[it, d, 1], row_in.at[it, d, 1])
        elif dx == 0:
            pairs[0] = (row_out.at[it, d, 0], row_in.at[it, d, 0])
        elif dy == 0:
            pairs[0] = (pack_out.at[it, d - 2], pack_in.at[it, d - 2])
        else:
            start = rows - 16 if dy > 0 else 0
            pairs[0] = (pack_out.at[it, 0 if dx > 0 else 1, start : start + 16], corner_in.at[it, d - 4])
        if it == 0 and not late:
            at = {1: slice(cols - lanes, cols), -1: slice(0, lanes), 0: slice(0, cols)}[dx]
            pairs[1] = (own_tiss.at[:, at], near_tiss.at[d, :, at])
        return [
            pltpu.make_async_remote_copy(
                src_ref=a,
                dst_ref=b,
                send_sem=halo_send.at[it, d, j],
                recv_sem=halo_recv.at[it, d, j],
                device_id={"gy": gy + dy, "gx": gx + dx},
                device_id_type=MESH,
            )
            for j, (a, b) in pairs.items()
        ]

    def clear_missing(it):
        for d, (dy, dx) in enumerate(DIRS):

            @pl.when(jnp.logical_not(exists(-dy, -dx)))
            def _():
                if dx == 0:
                    rows_in[it, d] = jnp.zeros(rows_in.shape[2:], jnp.float32)
                    row_in[it, d] = jnp.zeros(row_in.shape[2:], jnp.float32)
                elif dy == 0:
                    pack_in[it, d - 2] = jnp.zeros(pack_in.shape[2:], jnp.float32)
                else:
                    corner_in[it, d - 4] = jnp.zeros(corner_in.shape[2:], jnp.float32)
                if it == 0:
                    near_tiss[d] = jnp.zeros(near_tiss.shape[1:], jnp.float32)

    def start_halo(src, it):
        for late in (False, True):
            for d, (dy, dx) in enumerate(DIRS[:2] if late else DIRS):

                @pl.when(exists(dy, dx))
                def _():
                    for copy in copies(src, it, d, late):
                        copy.start()

    def wait_halo(src, it, late):
        for d, (dy, dx) in enumerate(DIRS[:2] if late else DIRS):

            @pl.when(exists(-dy, -dx))
            def _():
                for copy in copies(src, it, d, late):
                    copy.wait_recv()

    def wait_sent(src, it):
        for d, (dy, dx) in enumerate(DIRS):

            @pl.when(exists(dy, dx))
            def _():
                for late in (False, True):
                    for copy in copies(src, it, d, late):
                        copy.wait_send()

    def sum_copies(axis):
        count, buffer = (nx, row_sums) if axis == "gx" else (ny, col_sums)
        stage = 0 if axis == "gx" else 1
        return [
            pltpu.make_async_remote_copy(
                src_ref=buffer.at[0],
                dst_ref=buffer.at[k],
                send_sem=sum_send.at[stage, k],
                recv_sem=sum_recv.at[stage, k],
                device_id=peer(axis, k),
                device_id_type=MESH,
            )
            for k in range(1, count)
        ]

    def spread(ref, index, flags):
        for k in range(nb + 2):
            ref[index + (slice(8 * k, 8 * k + 8),)] = jnp.broadcast_to(flags[k : k + 1], (8, lanes))

    def spread_tissue():
        lane = lane_of(8)
        spot = lane % 16
        inner = jnp.logical_and(lane > 0, lane < lanes - 1)
        valid = jnp.logical_or(
            jnp.logical_and(spot >= 1, spot <= 9), jnp.logical_and(spot >= 12, spot <= 14)
        )
        patterns = {}
        for zb in range(blocks_z):
            first = zb * blocks_y
            wide_tiss[zb, 1 : 1 + blocks_y, lanes : lanes + cols] = own_tiss[first : first + blocks_y]
            wide_tiss[zb, 1 : 1 + blocks_y, 0:lanes] = near_tiss[2, first : first + blocks_y, cols - lanes : cols]
            wide_tiss[zb, 1 : 1 + blocks_y, lanes + cols :] = near_tiss[3, first : first + blocks_y, 0:lanes]
            for row, source, at in ((0, (0, 4, 5), first + blocks_y - 1), (1 + blocks_y, (1, 6, 7), first)):
                mid_d, left_d, right_d = source
                wide_tiss[zb, row : row + 1, lanes : lanes + cols] = near_tiss[mid_d, at : at + 1, :]
                wide_tiss[zb, row : row + 1, 0:lanes] = near_tiss[left_d, at : at + 1, cols - lanes : cols]
                wide_tiss[zb, row : row + 1, lanes + cols :] = near_tiss[right_d, at : at + 1, 0:lanes]
            for ci in range(2):
                c = 8 * ci
                for t in range(2):
                    off = lanes + step * t + c
                    flags = (wide_tiss[zb, 0:8, off : off + lanes] - 1.0) * BIG
                    if ci == 0:
                        flags = jnp.where(inner, flags, -BIG)
                    spread(pens, (ci, t, zb), flags)
                left = wide_tiss[zb, 0:8, lanes - 9 + c : 2 * lanes - 9 + c]
                off = lanes + 2 * step + c - 11
                right = wide_tiss[zb, 0:8, off : off + lanes]
                part = jnp.where(lane < 11, left, jnp.where(lane < 16, right, 0.0))
                for shift in (16, 32, 64):
                    part = part + roll(part, shift)
                patterns[zb, ci] = (part - 1.0) * BIG
        low = lane < lanes // 2
        both = [jnp.where(low, patterns[0, ci], patterns[1, ci]) for ci in range(2)]
        own = jnp.where(valid, both[0], -BIG)
        spread(ppens, (0,), own)
        spread(ppens, (1,), both[1])
        spread(ppens, (2,), jnp.where(low, own, -BIG))
        spread(ppens, (3,), patterns[1, 0])
        spread(ppens, (4,), patterns[1, 1])
        spread(ppens, (5,), jnp.where(low, -BIG, own))
        spread(ppens, (6,), patterns[0, 1])
        spread(ppens, (7,), patterns[0, 0])

    def shifted(n0, n1, extra):
        lane = lane_of(n0.shape[0])
        return (
            n0,
            jnp.where(lane < 2, roll(n0, 2), roll(n1, 2)),
            jnp.where(lane < lanes - 8, roll(n0, -8), roll(n1, -8)),
            roll(n1, -6) if extra is None else jnp.where(lane < lanes - 6, roll(n1, -6), extra),
        )

    def fill_own(src):
        for z in range(depth):
            four = shifted(src[z, :, 0:lanes], src[z, :, lanes : 2 * lanes], None)
            for k, part in enumerate(four):
                vals[k // 2, k % 2, z, PAD : PAD + rows] = part

    def fill_line(it, d, which, corner, at):
        line = jnp.broadcast_to(corner_in[it, 2 * d + 1, corner : corner + 1], (depth, lanes))
        extra = pltpu.roll(line, 10, 1, stride=16, stride_axis=0)
        single = row_in[it, d, which]
        four = shifted(single[:, 0:lanes], single[:, lanes : 2 * lanes], None)
        for k, part in enumerate(four):
            for z in range(depth):
                row = part[z : z + 1]
                if k == 3:
                    row = jnp.where(lane_of(1) < lanes - 6, row, extra[depth - 1 - z : depth - z])
                vals[k // 2, k % 2, z, at : at + 1] = row
        fill_packs(
            at, corner_in[it, 2 * d, corner : corner + 1], packed_line(single),
            corner_in[it, 2 * d + 1, corner : corner + 1],
        )

    def fill_early(it):
        lane = lane_of(rows)
        for z in range(depth):
            extra = roll(pack_in[it, 1], lanes - 6 - 16 * z)
            vals[1, 1, z, PAD : PAD + rows] = jnp.where(
                lane < lanes - 6, vals[1, 1, z, PAD : PAD + rows], extra
            )
        fill_packs(PAD, pack_in[it, 0], (pack_out[it, 1], pack_out[it, 0]), pack_in[it, 1])
        fill_line(it, 0, 0, 15, PAD - 1)
        fill_line(it, 1, 0, 0, PAD + rows)
        fill_squares()

    def fill_late(it):
        for d, at, single, alone in ((0, 8, 7, PAD - 9), (1, 0, 8, PAD + rows + 8)):
            start = PAD - 8 if d == 0 else PAD + rows
            for z in range(depth):
                extra = roll(corner_in[it, 2 * d + 1, at : at + 8], lanes - 6 - 16 * z)
                four = shifted(rows_in[it, d, z, :, 0:lanes], rows_in[it, d, z, :, lanes : 2 * lanes], extra)
                for k, part in enumerate(four):
                    vals[k // 2, k % 2, z, start : start + 8] = part
            fill_line(it, d, 1, single, alone)
            fill_packs(
                start, corner_in[it, 2 * d, at : at + 8], packed([rows_in[it, d, z] for z in range(depth)]),
                corner_in[it, 2 * d + 1, at : at + 8],
            )
        fill_squares()

    def fill_packs(start, right_of_left, own, left_of_right):
        left, right = own
        size = left.shape[0]
        lane = lane_of(size)
        spot, group = lane % 16, lane // 16
        zero = jnp.where(
            spot < 9,
            right_of_left,
            jnp.where(
                spot < 11, roll(left, 9), jnp.where(spot < 15, roll(right, 6), roll(left_of_right, 15))
            ),
        )
        eight = jnp.where(
            spot < 1, roll(right_of_left, -8), jnp.where(spot < 11, roll(left, 1), roll(left_of_right, 7))
        )
        hole = jnp.logical_and(group >= 4, group < 7)
        gap = jnp.logical_and(group >= 1, group < 4)
        half_zero, half_eight = roll(zero, 64), roll(eight, 64)
        at = slice(start, start + size)
        packs[0, at] = zero
        packs[1, at] = eight
        packs[2, at] = jnp.where(group == 7, 0.0, zero)
        packs[3, at] = jnp.where(hole, 0.0, half_zero)
        packs[4, at] = jnp.where(hole, 0.0, half_eight)
        packs[5, at] = jnp.where(group == 0, 0.0, zero)
        packs[6, at] = jnp.where(gap, 0.0, half_eight)

    def fill_squares():
        for t in range(2):
            for ci in range(2):
                for k in range(2):
                    plane = vals[ci, t, depth // 2 - 1 + k]
                    squares[k, ci, t] = plane * plane

    def extent(b):
        k0 = -1 if b > 0 else 0
        k1 = nb + 1 if b < 0 else nb
        return k0, k1, PAD + 8 * (k0 - 1), 8 * (k1 - k0 + 2)

    def add(ref, index, value, init):
        ref[index] = value if init else ref[index] + value

    def box(parts, kind=0):
        tops = [part.astype(jnp.bfloat16).astype(jnp.float32) for part in parts]
        lhs = [jnp.concatenate([top, part - top], axis=1) for part, top in zip(parts, tops)]
        return jnp.dot(jnp.concatenate(lhs, axis=0), band[kind], preferred_element_type=jnp.float32)

    def main_offset(t, offset, init, scale, slot, mode):
        a, b, c = offset
        ci, bb = c // 8, b // 8
        k0, k1, lo, size = extent(b)
        inner = size - 16
        low, planes = max(0, -a), depth - abs(a)
        high = low + planes

        def differ(z, low_row, count):
            far = slice(low_row + b, low_row + b + count)
            return vals[ci, t, z + a, far] - vals[0, t, z, low_row : low_row + count]

        def outside(z):
            if a == 0:
                return None
            if (z < low) == (a > 0):
                return squares[0 if a > 0 else 1, ci, t, lo + b : lo + b + size]
            return squares[1 if a > 0 else 0, 0, t, lo : lo + size]

        own_pen, far_pen = slice(8 * (k0 + 1), 8 * (k1 + 1)), slice(8 * (k0 + bb + 1), 8 * (k1 + bb + 1))
        po, qo = -8 * k0, -8 * (bb + k0)
        penalty = None
        before = None
        diffs, sqs = {}, {}
        queue = []

        def grow(z):
            diffs[z] = differ(z, lo, size)
            sqs[z] = diffs[z] * diffs[z]

        if mode != "apply":
            before = outside(low - 1)
            grow(low)
        for z in range(low, high, 2):
            if z % 4 == 0 and mode != "measure":
                penalty = pens[0, t, z // 4, own_pen] + pens[ci, t, (z + a) // 4, far_pen]
            cubed = (None, None)
            if mode != "apply":
                grow(z + 1)
                pair = sqs[z] + sqs[z + 1]
                if z + 2 < high:
                    grow(z + 2)
                    after = sqs[z + 2]
                else:
                    after = outside(high)
                cubed = (
                    pair if before is None else pair + before,
                    pair if after is None else pair + after,
                )
                before = sqs[z + 1]
            for plane, cube in zip((z, z + 1), cubed):
                if mode != "apply":
                    at = slot % SLOTS
                    cubes[at, 0:size] = cube
                    total = cube[8 : 8 + inner] + cubes[at, 7 : 7 + inner] + cubes[at, 9 : 9 + inner]
                    if mode == "measure":
                        slot += 1
                        queue.append(total)
                        continue
                    total = total + roll(total, 1) + roll(total, -1)
                if mode == "apply":
                    total = totals[t, slot, 0:inner]
                    gap = differ(plane, lo + 8, inner)
                else:
                    gap = diffs[plane][8 : 8 + inner]
                slot += 1
                weight = jnp.exp2(penalty - (total if scale is None else total * scale[0:inner]))
                push = weight * gap
                add(acc, (0, 0, t, plane), push[po : po + rows], init)
                add(acc, (0, 1, t, plane), weight[po : po + rows], init)
                far = plane + a
                if init:
                    acc[ci, 0, t, far] = -push[qo : qo + rows]
                else:
                    acc[ci, 0, t, far] -= push[qo : qo + rows]
                add(acc, (ci, 1, t, far), weight[qo : qo + rows], init)
        if mode == "measure":
            summed = box(queue)
            for k in range(len(queue)):
                totals[t, slot - len(queue) + k, 0:inner] = summed[k * inner : (k + 1) * inner]
        return slot

    order = [offset for offset in LEVEL + CROSS if offset[1] == 0]
    flat = len(order)
    order += [offset for offset in LEVEL + CROSS if offset[1] != 0]
    bases = [sum(depth - abs(other[0]) for other in order[:k]) for k in range(len(order))]

    def main_gather(jobs, scale, mode):
        def body(t, carry):
            for k in jobs:
                main_offset(t, order[k], k == 0, scale, bases[k], mode)
            return carry

        lax.fori_loop(0, 2, body, 0)

    packed_items = []
    for a, b, c in LEVEL + CROSS:
        near, far = {0: (0, c // 8), 4: (2, 3 + c // 8), -4: (5, 6)}[a]
        packed_items.append((near, far, b, c // 8 + 2 * (a != 0), a == 0))

    def pack_differ(near, far, b, low, size):
        return packs[far, low + b : low + b + size] - packs[near, low : low + size]

    def pack_measure():
        for k, (near, far, b, key, masked) in enumerate(packed_items):
            lo, size = extent(b)[2:]
            gap = pack_differ(near, far, b, lo, size)
            pcubes[k, 0:size] = gap * gap
        for kind in range(2):
            chosen = [(k, item) for k, item in enumerate(packed_items) if item[4] == (kind == 0)]
            parts = []
            for k, item in chosen:
                inner = extent(item[2])[3] - 16
                parts.append(pcubes[k, 7 : 7 + inner] + pcubes[k, 8 : 8 + inner] + pcubes[k, 9 : 9 + inner])
            pooled = box(parts, 1 + kind)
            at = 0
            for (k, item), part in zip(chosen, parts):
                found[k, 0 : part.shape[0]] = pooled[at : at + part.shape[0]]
                at += part.shape[0]

    def pack_apply(scale):
        parts = [[None] * 4, [None] * 4]

        def gain(kind, key, value, minus):
            old = parts[kind][key]
            if old is None:
                parts[kind][key] = -value if minus else value
            else:
                parts[kind][key] = old - value if minus else old + value

        for k, (near, far, b, key, masked) in enumerate(packed_items):
            k0, k1, lo, size = extent(b)
            bb, inner = b // 8, size - 16
            penalty = ppens[near, 8 * (k0 + 1) : 8 * (k1 + 1)] + ppens[far, 8 * (k0 + bb + 1) : 8 * (k1 + bb + 1)]
            total = found[k, 0:inner]
            weight = jnp.exp2(penalty - (total if scale is None else total * scale[0:inner]))
            push = weight * pack_differ(near, far, b, lo + 8, inner)
            po, qo = -8 * k0, -8 * (bb + k0)
            gain(0, 0, push[po : po + rows], False)
            gain(1, 0, weight[po : po + rows], False)
            gain(0, key, push[qo : qo + rows], True)
            gain(1, key, weight[qo : qo + rows], False)
        return parts

    def merge(parts):
        lane = lane_of(rows)
        spot = lane % 16
        merged = []
        for kind in range(2):
            zero = parts[kind][0] + roll(parts[kind][2], 64)
            eight = parts[kind][1] + roll(parts[kind][3], 64)
            eight = eight + jnp.where(spot == 1, roll(zero, -8), 0.0)
            merged.append(
                jnp.where(jnp.logical_or(spot >= 14, spot == 0), roll(zero, -14), jnp.where(spot < 10, eight, 0.0))
            )
        return merged

    def finish(src, dst, merged, factor):
        lane = lane_of(rows)
        for z in range(depth):
            sides = []
            for kind in range(2):
                near = roll(merged[kind], -(16 * z + 1))
                first = acc[0, kind, 0, z]
                second = roll(acc[0, kind, 1, z], -2)
                far_first = roll(acc[1, kind, 0, z], 8)
                far_second = roll(acc[1, kind, 1, z], 6)
                sides.append((
                    first + jnp.where(lane < 9, near, far_first) + jnp.where(lane == lanes - 1, second, 0.0),
                    jnp.where(lane >= lanes - 3, near, second) + jnp.where(lane < 7, far_first, far_second),
                ))
            for t in range(2):
                at = slice(t * lanes, (t + 1) * lanes)
                dst[z, :, at] = (src[z, :, at] + sides[0][t] / (sides[1][t] + 1.0)) * factor

    row_at = lax.broadcasted_iota(jnp.int32, (2 * lanes, lanes), 0) % lanes
    col_at = lax.broadcasted_iota(jnp.int32, (2 * lanes, lanes), 1)
    beside = jnp.abs(row_at % 16 - col_at % 16) <= 1
    apart = jnp.abs(row_at // 16 - col_at // 16)
    for kind, rule in enumerate((
        jnp.abs(row_at - col_at) <= 1,
        jnp.logical_and(beside, apart <= 1),
        jnp.logical_and(beside, jnp.logical_or(apart <= 1, apart == depth - 1)),
    )):
        band[kind] = rule.astype(jnp.float32)
    loads[0].wait()
    widen = (
        lax.broadcasted_iota(jnp.int32, (blocks_x, cols), 1) // 8
        == lax.broadcasted_iota(jnp.int32, (blocks_x, cols), 0)
    ).astype(jnp.float32)
    for zb in range(blocks_z):
        flags = mask_ref[zb].astype(jnp.float32)
        own_tiss[zb * blocks_y : (zb + 1) * blocks_y] = jnp.dot(
            flags, widen, preferred_element_type=jnp.float32
        )
    loads[1].wait()
    total = jnp.zeros((8, cols), jnp.float32)
    count = jnp.zeros((8, cols), jnp.float32)
    for z in range(1, depth - 1):
        residual = vol_ref[z] - 0.5 * (vol_ref[z - 1] + vol_ref[z + 1])
        for yb in range(blocks_y):
            line = (z // 4) * blocks_y + yb
            flag = jnp.broadcast_to(own_tiss[line : line + 1], (8, cols))
            piece = residual[8 * yb : 8 * yb + 8]
            total = total + flag * piece * piece
            count = count + flag
    total = jnp.sum(total, axis=0, keepdims=True)
    count = jnp.sum(count, axis=0, keepdims=True)
    tiles = cols // lanes
    total = functools.reduce(jnp.add, [total[:, i * lanes : (i + 1) * lanes] for i in range(tiles)])
    count = functools.reduce(jnp.add, [count[:, i * lanes : (i + 1) * lanes] for i in range(tiles)])
    lane = lax.broadcasted_iota(jnp.int32, (1, lanes), 1)
    row_sums[0] = jnp.where(
        lane < lanes // 2,
        jnp.sum(total, axis=1, keepdims=True),
        jnp.sum(count, axis=1, keepdims=True),
    )
    make_packs(vol_ref, 0)
    pl.semaphore_wait(barrier, nx - 1 + present(others))
    rounds = known.shape[0]
    for copy in sum_copies("gx"):
        copy.start()
    greet(known.at[0], column)
    start_halo(vol_ref, 0)
    for it in range(ITERS):
        clear_missing(it)
    fill_own(vol_ref)
    for k in range(rounds):
        pl.semaphore_wait(known.at[k], present(column))
        if k + 1 < rounds:
            greet(known.at[k + 1], column)
    for copy in sum_copies("gx"):
        copy.wait_recv()
    col_sums[0] = functools.reduce(jnp.add, [row_sums[k] for k in range(nx)])
    for copy in sum_copies("gy"):
        copy.start()
    wait_halo(vol_ref, 0, False)
    spread_tissue()
    fill_early(0)
    main_gather(range(flat), None, "measure")
    wait_halo(vol_ref, 0, True)
    fill_late(0)
    pack_measure()
    main_gather(range(flat, len(order)), None, "measure")
    for copy in sum_copies("gy"):
        copy.wait_recv()
    everything = functools.reduce(jnp.add, [col_sums[k] for k in range(ny)])
    summed = everything[:, 0:1] * (2.0 / 3.0)
    tissue_count = everything[:, lanes // 2 : lanes // 2 + 1]
    variance = summed / jnp.maximum(tissue_count, 1.0) + 1e-05
    width = 54.0 * smooth_ref[0] * smooth_ref[0]
    power = LOG2E / (width * variance)
    scale = jnp.broadcast_to(power, (rows + 8, lanes))
    root = jnp.broadcast_to(jnp.sqrt(power), (rows, lanes))
    inverse = jnp.broadcast_to(1.0 / jnp.sqrt(power), (rows, lanes))
    merged = merge(pack_apply(scale))
    main_gather(range(len(order)), scale, "apply")
    finish(vol_ref, mid, merged, root)
    make_packs(mid, 1)
    start_halo(mid, 1)
    fill_own(mid)
    wait_halo(mid, 1, False)
    fill_early(1)
    main_gather(range(flat), None, "both")
    wait_halo(mid, 1, True)
    fill_late(1)
    pack_measure()
    merged = merge(pack_apply(None))
    main_gather(range(flat, len(order)), None, "both")
    finish(mid, out_ref, merged, inverse)
    wait_sent(vol_ref, 0)
    wait_sent(mid, 1)
    for axis in ("gx", "gy"):
        for copy in sum_copies(axis):
            copy.wait_send()


def on_device(volume, tissue_mask, smoothing):
    ny, nx = lax.axis_size("gy"), lax.axis_size("gx")
    depth, rows, cols = volume.shape
    blocks_z, blocks_y, blocks_x = tissue_mask.shape
    lanes = 128
    assert depth == 8 and cols == 2 * lanes and blocks_z == 2
    flag_rows = -(-(blocks_y + 2) // 8) * 8
    f32 = jnp.float32
    vmem = pl.BlockSpec(memory_space=pltpu.VMEM)
    anywhere = pl.BlockSpec(memory_space=pltpu.HBM)
    return pl.pallas_call(
        functools.partial(kernel, ny, nx),
        out_shape=jax.ShapeDtypeStruct(volume.shape, f32),
        in_specs=[pl.BlockSpec(memory_space=pltpu.SMEM), anywhere, anywhere],
        out_specs=vmem,
        scratch_shapes=[
            pltpu.VMEM((depth, rows, cols), f32),
            pltpu.VMEM((blocks_z, blocks_y, blocks_x), jnp.int32),
            pltpu.VMEM((depth, rows, cols), f32),
            pltpu.VMEM((2, 2, depth, rows + 2 * PAD, lanes), f32),
            pltpu.VMEM((7, rows + 2 * PAD, lanes), f32),
            pltpu.VMEM((2, 2, 2, rows + 2 * PAD, lanes), f32),
            pltpu.VMEM((SLOTS, rows + 24, lanes), f32),
            pltpu.VMEM((2, len(LEVEL) * depth + len(CROSS) * depth // 2, rows + 8, lanes), f32),
            pltpu.VMEM((3, 2 * lanes, lanes), f32),
            pltpu.VMEM((2, 2, 2, depth, rows, lanes), f32),
            pltpu.VMEM((13, rows + 24, lanes), f32),
            pltpu.VMEM((13, rows + 8, lanes), f32),
            pltpu.VMEM((2, 2, blocks_z, rows + 16, lanes), f32),
            pltpu.VMEM((8, rows + 16, lanes), f32),
            pltpu.VMEM((blocks_z * blocks_y, cols), f32),
            pltpu.VMEM((len(DIRS), blocks_z * blocks_y, cols), f32),
            pltpu.VMEM((blocks_z, flag_rows, cols + 2 * lanes), f32),
            pltpu.VMEM((ITERS, 2, depth, 8, cols), f32),
            pltpu.VMEM((ITERS, 2, 2, depth, cols), f32),
            pltpu.VMEM((ITERS, 2, 2, depth, cols), f32),
            pltpu.VMEM((ITERS, 2, rows, lanes), f32),
            pltpu.VMEM((ITERS, 2, rows, lanes), f32),
            pltpu.VMEM((ITERS, 4, 16, lanes), f32),
            pltpu.VMEM((nx, 1, lanes), f32),
            pltpu.VMEM((ny, 1, lanes), f32),
            pltpu.SemaphoreType.DMA((2,)),
            pltpu.SemaphoreType.REGULAR((max((ny - 2) // 2, 1),)),
            pltpu.SemaphoreType.DMA((2, max(ny, nx))),
            pltpu.SemaphoreType.DMA((2, max(ny, nx))),
            pltpu.SemaphoreType.DMA((ITERS, len(DIRS), 4)),
            pltpu.SemaphoreType.DMA((ITERS, len(DIRS), 4)),
        ],
        compiler_params=pltpu.CompilerParams(
            collective_id=0, has_side_effects=True, vmem_limit_bytes=16 * 2**20
        ),
    )(
        smoothing,
        pltpu.with_memory_space_constraint(volume, pltpu.HBM),
        pltpu.with_memory_space_constraint(tissue_mask, pltpu.HBM),
    )


def solution(mesh):
    placed = (P(None, ("slab", "gy"), "gx"), P(None, ("slab", "gy"), "gx"), P())
    return jax.shard_map(
        on_device,
        mesh=mesh,
        in_specs=placed,
        out_specs=P(None, ("slab", "gy"), "gx"),
        check_vma=False,
    )
```

```python
import functools

import jax
import jax.numpy as jnp
from jax import lax
from jax.experimental import pallas as pl
from jax.experimental.pallas import tpu as pltpu
from jax.sharding import PartitionSpec as P

MESH = pl.DeviceIdType.MESH
ITERS = 2
LOG2E = 1.4426950408889634
BIG = 1e30
DIRS = ((1, 0), (-1, 0), (0, 1), (0, -1), (1, 1), (1, -1), (-1, 1), (-1, -1))
LEVEL = ((0, 0, 8), (0, 8, 8), (0, -8, 8), (0, 8, 0))
CROSS = (
    (4, 0, 8), (4, 8, 8), (4, -8, 8), (-4, 0, 8), (-4, 8, 8), (-4, -8, 8), (4, 0, 0), (4, 8, 0), (4, -8, 0)
)
PAD = 16
SLOTS = 96


def kernel(
    ny, nx, smooth_ref, vol_hbm, mask_hbm, out_ref, vol_ref, mask_ref, mid, vals, packs, squares,
    cubes, totals, band, acc, pcubes, found, pens, ppens, own_tiss, near_tiss, wide_tiss,
    rows_in, row_in, row_out, pack_out, pack_in, corner_in, row_sums, col_sums,
    load_sem, known, sum_send, sum_recv, halo_send, halo_recv,
):
    depth, rows, cols = vol_ref.shape
    lanes = 128
    blocks_z, blocks_y, blocks_x = mask_ref.shape
    nb = rows // 8
    step = lanes - 2
    gy, gx = lax.axis_index("gy"), lax.axis_index("gx")

    barrier = pltpu.get_barrier_semaphore()

    def exists(dy, dx):
        found = None
        for move, pos, count in ((dy, gy, ny), (dx, gx, nx)):
            if move == 0:
                continue
            here = pos < count - move if move > 0 else pos >= -move
            found = here if found is None else jnp.logical_and(found, here)
        return found

    def peer(axis, k):
        pos, count = (gy, ny) if axis == "gy" else (gx, nx)
        return {axis: jnp.where(pos + k >= count, pos + k - count, pos + k)}

    def greet(semaphore, moves):
        for dy, dx in moves:

            @pl.when(exists(dy, dx))
            def _():
                pl.semaphore_signal(
                    semaphore, inc=1, device_id={"gy": gy + dy, "gx": gx + dx}, device_id_type=MESH
                )

    def present(moves):
        return functools.reduce(jnp.add, [exists(dy, dx).astype(jnp.int32) for dy, dx in moves])

    column = [(dy, 0) for dy in (1, -1, 2, -2)]
    others = column + list(DIRS[4:])
    for k in range(1, nx):
        pl.semaphore_signal(barrier, inc=1, device_id=peer("gx", k), device_id_type=MESH)
    greet(barrier, others)

    loads = [
        pltpu.make_async_copy(mask_hbm, mask_ref, load_sem.at[0]),
        pltpu.make_async_copy(vol_hbm, vol_ref, load_sem.at[1]),
    ]
    for load in loads:
        load.start()

    def lane_of(n):
        return lax.broadcasted_iota(jnp.int32, (n, lanes), 1)

    def roll(x, shift):
        shift = shift % lanes
        return pltpu.roll(x, shift, 1) if shift else x

    def packed(planes):
        group = lane_of(planes[0].shape[0]) // 16
        left, right = planes[0][:, 0:lanes], roll(planes[0][:, cols - lanes : cols], 9)
        for z in range(1, depth):
            right = jnp.where(group == z, roll(planes[z][:, cols - lanes : cols], 16 * z + 9), right)
            left = jnp.where(group == z, roll(planes[z][:, 0:lanes], 16 * z), left)
        return left, right

    def packed_line(line):
        match = lane_of(depth) // 16 == lax.broadcasted_iota(jnp.int32, (depth, lanes), 0)
        ends = []
        for at, shift in ((0, 0), (cols - lanes, 9)):
            moved = pltpu.roll(line[:, at : at + lanes], shift, 1, stride=16, stride_axis=0)
            ends.append(jnp.sum(jnp.where(match, moved, 0.0), axis=0, keepdims=True))
        return ends

    def make_packs(src, it):
        for z in range(depth):
            for d, first, ninth in ((0, rows - 1, rows - 9), (1, 0, 8)):
                row_out[it, d, 0, z : z + 1] = src[z, first : first + 1, :]
                row_out[it, d, 1, z : z + 1] = src[z, ninth : ninth + 1, :]
        left, right = packed([src[z] for z in range(depth)])
        pack_out[it, 0] = right
        pack_out[it, 1] = left

    def copies(src, it, d, late):
        dy, dx = DIRS[d]
        pairs = {}
        if late:
            if dx == 0:
                start = rows - 8 if dy > 0 else 0
                pairs[2] = (src.at[:, start : start + 8, :], rows_in.at[it, d])
                pairs[3] = (row_out.at[it, d, 1], row_in.at[it, d, 1])
        elif dx == 0:
            pairs[0] = (row_out.at[it, d, 0], row_in.at[it, d, 0])
        elif dy == 0:
            pairs[0] = (pack_out.at[it, d - 2], pack_in.at[it, d - 2])
        else:
            start = rows - 16 if dy > 0 else 0
            pairs[0] = (pack_out.at[it, 0 if dx > 0 else 1, start : start + 16], corner_in.at[it, d - 4])
        if it == 0 and not late:
            at = {1: slice(cols - lanes, cols), -1: slice(0, lanes), 0: slice(0, cols)}[dx]
            pairs[1] = (own_tiss.at[:, at], near_tiss.at[d, :, at])
        return [
            pltpu.make_async_remote_copy(
                src_ref=a,
                dst_ref=b,
                send_sem=halo_send.at[it, d, j],
                recv_sem=halo_recv.at[it, d, j],
                device_id={"gy": gy + dy, "gx": gx + dx},
                device_id_type=MESH,
            )
            for j, (a, b) in pairs.items()
        ]

    def clear_missing(it):
        for d, (dy, dx) in enumerate(DIRS):

            @pl.when(jnp.logical_not(exists(-dy, -dx)))
            def _():
                if dx == 0:
                    rows_in[it, d] = jnp.zeros(rows_in.shape[2:], jnp.float32)
                    row_in[it, d] = jnp.zeros(row_in.shape[2:], jnp.float32)
                elif dy == 0:
                    pack_in[it, d - 2] = jnp.zeros(pack_in.shape[2:], jnp.float32)
                else:
                    corner_in[it, d - 4] = jnp.zeros(corner_in.shape[2:], jnp.float32)
                if it == 0:
                    near_tiss[d] = jnp.zeros(near_tiss.shape[1:], jnp.float32)

    def start_halo(src, it):
        for late in (False, True):
            for d, (dy, dx) in enumerate(DIRS[:2] if late else DIRS):

                @pl.when(exists(dy, dx))
                def _():
                    for copy in copies(src, it, d, late):
                        copy.start()

    def wait_halo(src, it, late):
        for d, (dy, dx) in enumerate(DIRS[:2] if late else DIRS):

            @pl.when(exists(-dy, -dx))
            def _():
                for copy in copies(src, it, d, late):
                    copy.wait_recv()

    def wait_sent(src, it):
        for d, (dy, dx) in enumerate(DIRS):

            @pl.when(exists(dy, dx))
            def _():
                for late in (False, True):
                    for copy in copies(src, it, d, late):
                        copy.wait_send()

    def sum_copies(axis):
        count, buffer = (nx, row_sums) if axis == "gx" else (ny, col_sums)
        stage = 0 if axis == "gx" else 1
        return [
            pltpu.make_async_remote_copy(
                src_ref=buffer.at[0],
                dst_ref=buffer.at[k],
                send_sem=sum_send.at[stage, k],
                recv_sem=sum_recv.at[stage, k],
                device_id=peer(axis, k),
                device_id_type=MESH,
            )
            for k in range(1, count)
        ]

    def spread(ref, index, flags):
        for k in range(nb + 2):
            ref[index + (slice(8 * k, 8 * k + 8),)] = jnp.broadcast_to(flags[k : k + 1], (8, lanes))

    def spread_tissue():
        lane = lane_of(8)
        spot = lane % 16
        inner = jnp.logical_and(lane > 0, lane < lanes - 1)
        valid = jnp.logical_or(
            jnp.logical_and(spot >= 1, spot <= 9), jnp.logical_and(spot >= 12, spot <= 14)
        )
        patterns = {}
        for zb in range(blocks_z):
            first = zb * blocks_y
            wide_tiss[zb, 1 : 1 + blocks_y, lanes : lanes + cols] = own_tiss[first : first + blocks_y]
            wide_tiss[zb, 1 : 1 + blocks_y, 0:lanes] = near_tiss[2, first : first + blocks_y, cols - lanes : cols]
            wide_tiss[zb, 1 : 1 + blocks_y, lanes + cols :] = near_tiss[3, first : first + blocks_y, 0:lanes]
            for row, source, at in ((0, (0, 4, 5), first + blocks_y - 1), (1 + blocks_y, (1, 6, 7), first)):
                mid_d, left_d, right_d = source
                wide_tiss[zb, row : row + 1, lanes : lanes + cols] = near_tiss[mid_d, at : at + 1, :]
                wide_tiss[zb, row : row + 1, 0:lanes] = near_tiss[left_d, at : at + 1, cols - lanes : cols]
                wide_tiss[zb, row : row + 1, lanes + cols :] = near_tiss[right_d, at : at + 1, 0:lanes]
            for ci in range(2):
                c = 8 * ci
                for t in range(2):
                    off = lanes + step * t + c
                    flags = (wide_tiss[zb, 0:8, off : off + lanes] - 1.0) * BIG
                    if ci == 0:
                        flags = jnp.where(inner, flags, -BIG)
                    spread(pens, (ci, t, zb), flags)
                left = wide_tiss[zb, 0:8, lanes - 9 + c : 2 * lanes - 9 + c]
                off = lanes + 2 * step + c - 11
                right = wide_tiss[zb, 0:8, off : off + lanes]
                part = jnp.where(lane < 11, left, jnp.where(lane < 16, right, 0.0))
                for shift in (16, 32, 64):
                    part = part + roll(part, shift)
                patterns[zb, ci] = (part - 1.0) * BIG
        low = lane < lanes // 2
        both = [jnp.where(low, patterns[0, ci], patterns[1, ci]) for ci in range(2)]
        own = jnp.where(valid, both[0], -BIG)
        spread(ppens, (0,), own)
        spread(ppens, (1,), both[1])
        spread(ppens, (2,), jnp.where(low, own, -BIG))
        spread(ppens, (3,), patterns[1, 0])
        spread(ppens, (4,), patterns[1, 1])
        spread(ppens, (5,), jnp.where(low, -BIG, own))
        spread(ppens, (6,), patterns[0, 1])
        spread(ppens, (7,), patterns[0, 0])

    def shifted(n0, n1, extra):
        lane = lane_of(n0.shape[0])
        return (
            n0,
            jnp.where(lane < 2, roll(n0, 2), roll(n1, 2)),
            jnp.where(lane < lanes - 8, roll(n0, -8), roll(n1, -8)),
            roll(n1, -6) if extra is None else jnp.where(lane < lanes - 6, roll(n1, -6), extra),
        )

    def fill_own(src):
        for z in range(depth):
            four = shifted(src[z, :, 0:lanes], src[z, :, lanes : 2 * lanes], None)
            for k, part in enumerate(four):
                vals[k // 2, k % 2, z, PAD : PAD + rows] = part

    def fill_line(it, d, which, corner, at):
        line = jnp.broadcast_to(corner_in[it, 2 * d + 1, corner : corner + 1], (depth, lanes))
        extra = pltpu.roll(line, 10, 1, stride=16, stride_axis=0)
        single = row_in[it, d, which]
        four = shifted(single[:, 0:lanes], single[:, lanes : 2 * lanes], None)
        for k, part in enumerate(four):
            for z in range(depth):
                row = part[z : z + 1]
                if k == 3:
                    row = jnp.where(lane_of(1) < lanes - 6, row, extra[depth - 1 - z : depth - z])
                vals[k // 2, k % 2, z, at : at + 1] = row
        fill_packs(
            at, corner_in[it, 2 * d, corner : corner + 1], packed_line(single),
            corner_in[it, 2 * d + 1, corner : corner + 1],
        )

    def fill_early(it):
        lane = lane_of(rows)
        for z in range(depth):
            extra = roll(pack_in[it, 1], lanes - 6 - 16 * z)
            vals[1, 1, z, PAD : PAD + rows] = jnp.where(
                lane < lanes - 6, vals[1, 1, z, PAD : PAD + rows], extra
            )
        fill_packs(PAD, pack_in[it, 0], (pack_out[it, 1], pack_out[it, 0]), pack_in[it, 1])
        fill_line(it, 0, 0, 15, PAD - 1)
        fill_line(it, 1, 0, 0, PAD + rows)
        fill_squares()

    def fill_late(it):
        for d, at, single, alone in ((0, 8, 7, PAD - 9), (1, 0, 8, PAD + rows + 8)):
            start = PAD - 8 if d == 0 else PAD + rows
            for z in range(depth):
                extra = roll(corner_in[it, 2 * d + 1, at : at + 8], lanes - 6 - 16 * z)
                four = shifted(rows_in[it, d, z, :, 0:lanes], rows_in[it, d, z, :, lanes : 2 * lanes], extra)
                for k, part in enumerate(four):
                    vals[k // 2, k % 2, z, start : start + 8] = part
            fill_line(it, d, 1, single, alone)
            fill_packs(
                start, corner_in[it, 2 * d, at : at + 8], packed([rows_in[it, d, z] for z in range(depth)]),
                corner_in[it, 2 * d + 1, at : at + 8],
            )
        fill_squares()

    def fill_packs(start, right_of_left, own, left_of_right):
        left, right = own
        size = left.shape[0]
        lane = lane_of(size)
        spot, group = lane % 16, lane // 16
        zero = jnp.where(
            spot < 9,
            right_of_left,
            jnp.where(
                spot < 11, roll(left, 9), jnp.where(spot < 15, roll(right, 6), roll(left_of_right, 15))
            ),
        )
        eight = jnp.where(
            spot < 1, roll(right_of_left, -8), jnp.where(spot < 11, roll(left, 1), roll(left_of_right, 7))
        )
        hole = jnp.logical_and(group >= 4, group < 7)
        gap = jnp.logical_and(group >= 1, group < 4)
        half_zero, half_eight = roll(zero, 64), roll(eight, 64)
        at = slice(start, start + size)
        packs[0, at] = zero
        packs[1, at] = eight
        packs[2, at] = jnp.where(group == 7, 0.0, zero)
        packs[3, at] = jnp.where(hole, 0.0, half_zero)
        packs[4, at] = jnp.where(hole, 0.0, half_eight)
        packs[5, at] = jnp.where(group == 0, 0.0, zero)
        packs[6, at] = jnp.where(gap, 0.0, half_eight)

    def fill_squares():
        for t in range(2):
            for ci in range(2):
                for k in range(2):
                    plane = vals[ci, t, depth // 2 - 1 + k]
                    squares[k, ci, t] = plane * plane

    def extent(b):
        k0 = -1 if b > 0 else 0
        k1 = nb + 1 if b < 0 else nb
        return k0, k1, PAD + 8 * (k0 - 1), 8 * (k1 - k0 + 2)

    def add(ref, index, value, init):
        ref[index] = value if init else ref[index] + value

    def box(parts, kind=0):
        tops = [part.astype(jnp.bfloat16).astype(jnp.float32) for part in parts]
        lhs = [jnp.concatenate([top, part - top], axis=1) for part, top in zip(parts, tops)]
        return jnp.dot(jnp.concatenate(lhs, axis=0), band[kind], preferred_element_type=jnp.float32)

    def main_offset(t, offset, init, scale, slot, mode):
        a, b, c = offset
        ci, bb = c // 8, b // 8
        k0, k1, lo, size = extent(b)
        inner = size - 16
        low, planes = max(0, -a), depth - abs(a)
        high = low + planes

        def differ(z, low_row, count):
            far = slice(low_row + b, low_row + b + count)
            return vals[ci, t, z + a, far] - vals[0, t, z, low_row : low_row + count]

        def outside(z):
            if a == 0:
                return None
            if (z < low) == (a > 0):
                return squares[0 if a > 0 else 1, ci, t, lo + b : lo + b + size]
            return squares[1 if a > 0 else 0, 0, t, lo : lo + size]

        own_pen, far_pen = slice(8 * (k0 + 1), 8 * (k1 + 1)), slice(8 * (k0 + bb + 1), 8 * (k1 + bb + 1))
        po, qo = -8 * k0, -8 * (bb + k0)
        penalty = None
        before = None
        diffs, sqs = {}, {}
        queue = []

        def grow(z):
            diffs[z] = differ(z, lo, size)
            sqs[z] = diffs[z] * diffs[z]

        if mode != "apply":
            before = outside(low - 1)
            grow(low)
        for z in range(low, high, 2):
            if z % 4 == 0 and mode != "measure":
                penalty = pens[0, t, z // 4, own_pen] + pens[ci, t, (z + a) // 4, far_pen]
            cubed = (None, None)
            if mode != "apply":
                grow(z + 1)
                pair = sqs[z] + sqs[z + 1]
                if z + 2 < high:
                    grow(z + 2)
                    after = sqs[z + 2]
                else:
                    after = outside(high)
                cubed = (
                    pair if before is None else pair + before,
                    pair if after is None else pair + after,
                )
                before = sqs[z + 1]
            for plane, cube in zip((z, z + 1), cubed):
                if mode != "apply":
                    at = slot % SLOTS
                    cubes[at, 0:size] = cube
                    total = cube[8 : 8 + inner] + cubes[at, 7 : 7 + inner] + cubes[at, 9 : 9 + inner]
                    if mode == "measure":
                        slot += 1
                        queue.append(total)
                        continue
                    total = total + roll(total, 1) + roll(total, -1)
                if mode == "apply":
                    total = totals[t, slot, 0:inner]
                    gap = differ(plane, lo + 8, inner)
                else:
                    gap = diffs[plane][8 : 8 + inner]
                slot += 1
                weight = jnp.exp2(penalty - (total if scale is None else total * scale[0:inner]))
                push = weight * gap
                add(acc, (0, 0, t, plane), push[po : po + rows], init)
                add(acc, (0, 1, t, plane), weight[po : po + rows], init)
                far = plane + a
                if init:
                    acc[ci, 0, t, far] = -push[qo : qo + rows]
                else:
                    acc[ci, 0, t, far] -= push[qo : qo + rows]
                add(acc, (ci, 1, t, far), weight[qo : qo + rows], init)
        if mode == "measure":
            summed = box(queue)
            for k in range(len(queue)):
                totals[t, slot - len(queue) + k, 0:inner] = summed[k * inner : (k + 1) * inner]
        return slot

    order = [offset for offset in LEVEL + CROSS if offset[1] == 0]
    flat = len(order)
    order += [offset for offset in LEVEL + CROSS if offset[1] != 0]
    bases = [sum(depth - abs(other[0]) for other in order[:k]) for k in range(len(order))]

    def main_gather(jobs, scale, mode):
        def body(t, carry):
            for k in jobs:
                if mode == "both" and k in (2, 4, 6, 8, 10, 12):
                    main_offset(t, order[k], k == 0, None, bases[k], "measure")
                    main_offset(t, order[k], k == 0, None, bases[k], "apply")
                else:
                    main_offset(t, order[k], k == 0, scale, bases[k], mode)
            return carry

        lax.fori_loop(0, 2, body, 0)

    packed_items = []
    for a, b, c in LEVEL + CROSS:
        near, far = {0: (0, c // 8), 4: (2, 3 + c // 8), -4: (5, 6)}[a]
        packed_items.append((near, far, b, c // 8 + 2 * (a != 0), a == 0))

    def pack_differ(near, far, b, low, size):
        return packs[far, low + b : low + b + size] - packs[near, low : low + size]

    def pack_measure():
        for k, (near, far, b, key, masked) in enumerate(packed_items):
            lo, size = extent(b)[2:]
            gap = pack_differ(near, far, b, lo, size)
            pcubes[k, 0:size] = gap * gap
        for kind in range(2):
            chosen = [(k, item) for k, item in enumerate(packed_items) if item[4] == (kind == 0)]
            parts = []
            for k, item in chosen:
                inner = extent(item[2])[3] - 16
                parts.append(pcubes[k, 7 : 7 + inner] + pcubes[k, 8 : 8 + inner] + pcubes[k, 9 : 9 + inner])
            pooled = box(parts, 1 + kind)
            at = 0
            for (k, item), part in zip(chosen, parts):
                found[k, 0 : part.shape[0]] = pooled[at : at + part.shape[0]]
                at += part.shape[0]

    def pack_apply(scale):
        parts = [[None] * 4, [None] * 4]

        def gain(kind, key, value, minus):
            old = parts[kind][key]
            if old is None:
                parts[kind][key] = -value if minus else value
            else:
                parts[kind][key] = old - value if minus else old + value

        for k, (near, far, b, key, masked) in enumerate(packed_items):
            k0, k1, lo, size = extent(b)
            bb, inner = b // 8, size - 16
            penalty = ppens[near, 8 * (k0 + 1) : 8 * (k1 + 1)] + ppens[far, 8 * (k0 + bb + 1) : 8 * (k1 + bb + 1)]
            total = found[k, 0:inner]
            weight = jnp.exp2(penalty - (total if scale is None else total * scale[0:inner]))
            push = weight * pack_differ(near, far, b, lo + 8, inner)
            po, qo = -8 * k0, -8 * (bb + k0)
            gain(0, 0, push[po : po + rows], False)
            gain(1, 0, weight[po : po + rows], False)
            gain(0, key, push[qo : qo + rows], True)
            gain(1, key, weight[qo : qo + rows], False)
        return parts

    def merge(parts):
        lane = lane_of(rows)
        spot = lane % 16
        merged = []
        for kind in range(2):
            zero = parts[kind][0] + roll(parts[kind][2], 64)
            eight = parts[kind][1] + roll(parts[kind][3], 64)
            eight = eight + jnp.where(spot == 1, roll(zero, -8), 0.0)
            merged.append(
                jnp.where(jnp.logical_or(spot >= 14, spot == 0), roll(zero, -14), jnp.where(spot < 10, eight, 0.0))
            )
        return merged

    def finish(src, dst, merged, factor):
        lane = lane_of(rows)
        for z in range(depth):
            sides = []
            for kind in range(2):
                near = roll(merged[kind], -(16 * z + 1))
                first = acc[0, kind, 0, z]
                second = roll(acc[0, kind, 1, z], -2)
                far_first = roll(acc[1, kind, 0, z], 8)
                far_second = roll(acc[1, kind, 1, z], 6)
                sides.append((
                    first + jnp.where(lane < 9, near, far_first) + jnp.where(lane == lanes - 1, second, 0.0),
                    jnp.where(lane >= lanes - 3, near, second) + jnp.where(lane < 7, far_first, far_second),
                ))
            for t in range(2):
                at = slice(t * lanes, (t + 1) * lanes)
                dst[z, :, at] = (src[z, :, at] + sides[0][t] / (sides[1][t] + 1.0)) * factor

    row_at = lax.broadcasted_iota(jnp.int32, (2 * lanes, lanes), 0) % lanes
    col_at = lax.broadcasted_iota(jnp.int32, (2 * lanes, lanes), 1)
    beside = jnp.abs(row_at % 16 - col_at % 16) <= 1
    apart = jnp.abs(row_at // 16 - col_at // 16)
    for kind, rule in enumerate((
        jnp.abs(row_at - col_at) <= 1,
        jnp.logical_and(beside, apart <= 1),
        jnp.logical_and(beside, jnp.logical_or(apart <= 1, apart == depth - 1)),
    )):
        band[kind] = rule.astype(jnp.float32)
    loads[0].wait()
    widen = (
        lax.broadcasted_iota(jnp.int32, (blocks_x, cols), 1) // 8
        == lax.broadcasted_iota(jnp.int32, (blocks_x, cols), 0)
    ).astype(jnp.float32)
    for zb in range(blocks_z):
        flags = mask_ref[zb].astype(jnp.float32)
        own_tiss[zb * blocks_y : (zb + 1) * blocks_y] = jnp.dot(
            flags, widen, preferred_element_type=jnp.float32
        )
    loads[1].wait()
    total = jnp.zeros((8, cols), jnp.float32)
    count = jnp.zeros((8, cols), jnp.float32)
    for z in range(1, depth - 1):
        residual = vol_ref[z] - 0.5 * (vol_ref[z - 1] + vol_ref[z + 1])
        for yb in range(blocks_y):
            line = (z // 4) * blocks_y + yb
            flag = jnp.broadcast_to(own_tiss[line : line + 1], (8, cols))
            piece = residual[8 * yb : 8 * yb + 8]
            total = total + flag * piece * piece
            count = count + flag
    total = jnp.sum(total, axis=0, keepdims=True)
    count = jnp.sum(count, axis=0, keepdims=True)
    tiles = cols // lanes
    total = functools.reduce(jnp.add, [total[:, i * lanes : (i + 1) * lanes] for i in range(tiles)])
    count = functools.reduce(jnp.add, [count[:, i * lanes : (i + 1) * lanes] for i in range(tiles)])
    lane = lax.broadcasted_iota(jnp.int32, (1, lanes), 1)
    row_sums[0] = jnp.where(
        lane < lanes // 2,
        jnp.sum(total, axis=1, keepdims=True),
        jnp.sum(count, axis=1, keepdims=True),
    )
    make_packs(vol_ref, 0)
    pl.semaphore_wait(barrier, nx - 1 + present(others))
    rounds = known.shape[0]
    for copy in sum_copies("gx"):
        copy.start()
    greet(known.at[0], column)
    start_halo(vol_ref, 0)
    for it in range(ITERS):
        clear_missing(it)
    fill_own(vol_ref)
    for k in range(rounds):
        pl.semaphore_wait(known.at[k], present(column))
        if k + 1 < rounds:
            greet(known.at[k + 1], column)
    for copy in sum_copies("gx"):
        copy.wait_recv()
    col_sums[0] = functools.reduce(jnp.add, [row_sums[k] for k in range(nx)])
    for copy in sum_copies("gy"):
        copy.start()
    wait_halo(vol_ref, 0, False)
    spread_tissue()
    fill_early(0)
    main_gather(range(flat), None, "measure")
    wait_halo(vol_ref, 0, True)
    fill_late(0)
    pack_measure()
    main_gather(range(flat, len(order)), None, "measure")
    for copy in sum_copies("gy"):
        copy.wait_recv()
    everything = functools.reduce(jnp.add, [col_sums[k] for k in range(ny)])
    summed = everything[:, 0:1] * (2.0 / 3.0)
    tissue_count = everything[:, lanes // 2 : lanes // 2 + 1]
    variance = summed / jnp.maximum(tissue_count, 1.0) + 1e-05
    width = 54.0 * smooth_ref[0] * smooth_ref[0]
    power = LOG2E / (width * variance)
    scale = jnp.broadcast_to(power, (rows + 8, lanes))
    root = jnp.broadcast_to(jnp.sqrt(power), (rows, lanes))
    inverse = jnp.broadcast_to(1.0 / jnp.sqrt(power), (rows, lanes))
    merged = merge(pack_apply(scale))
    main_gather(range(len(order)), scale, "apply")
    finish(vol_ref, mid, merged, root)
    make_packs(mid, 1)
    start_halo(mid, 1)
    fill_own(mid)
    wait_sent(vol_ref, 0)
    for axis in ("gx", "gy"):
        for copy in sum_copies(axis):
            copy.wait_send()
    wait_halo(mid, 1, False)
    fill_early(1)
    main_gather(range(flat), None, "both")
    wait_halo(mid, 1, True)
    fill_late(1)
    pack_measure()
    merged = merge(pack_apply(None))
    main_gather(range(flat, len(order)), None, "both")
    finish(mid, out_ref, merged, inverse)
    wait_sent(mid, 1)


def on_device(volume, tissue_mask, smoothing):
    ny, nx = lax.axis_size("gy"), lax.axis_size("gx")
    depth, rows, cols = volume.shape
    blocks_z, blocks_y, blocks_x = tissue_mask.shape
    lanes = 128
    assert depth == 8 and cols == 2 * lanes and blocks_z == 2
    flag_rows = -(-(blocks_y + 2) // 8) * 8
    f32 = jnp.float32
    vmem = pl.BlockSpec(memory_space=pltpu.VMEM)
    anywhere = pl.BlockSpec(memory_space=pltpu.HBM)
    return pl.pallas_call(
        functools.partial(kernel, ny, nx),
        out_shape=jax.ShapeDtypeStruct(volume.shape, f32),
        in_specs=[pl.BlockSpec(memory_space=pltpu.SMEM), anywhere, anywhere],
        out_specs=vmem,
        scratch_shapes=[
            pltpu.VMEM((depth, rows, cols), f32),
            pltpu.VMEM((blocks_z, blocks_y, blocks_x), jnp.int32),
            pltpu.VMEM((depth, rows, cols), f32),
            pltpu.VMEM((2, 2, depth, rows + 2 * PAD, lanes), f32),
            pltpu.VMEM((7, rows + 2 * PAD, lanes), f32),
            pltpu.VMEM((2, 2, 2, rows + 2 * PAD, lanes), f32),
            pltpu.VMEM((SLOTS, rows + 24, lanes), f32),
            pltpu.VMEM((2, len(LEVEL) * depth + len(CROSS) * depth // 2, rows + 8, lanes), f32),
            pltpu.VMEM((3, 2 * lanes, lanes), f32),
            pltpu.VMEM((2, 2, 2, depth, rows, lanes), f32),
            pltpu.VMEM((13, rows + 24, lanes), f32),
            pltpu.VMEM((13, rows + 8, lanes), f32),
            pltpu.VMEM((2, 2, blocks_z, rows + 16, lanes), f32),
            pltpu.VMEM((8, rows + 16, lanes), f32),
            pltpu.VMEM((blocks_z * blocks_y, cols), f32),
            pltpu.VMEM((len(DIRS), blocks_z * blocks_y, cols), f32),
            pltpu.VMEM((blocks_z, flag_rows, cols + 2 * lanes), f32),
            pltpu.VMEM((ITERS, 2, depth, 8, cols), f32),
            pltpu.VMEM((ITERS, 2, 2, depth, cols), f32),
            pltpu.VMEM((ITERS, 2, 2, depth, cols), f32),
            pltpu.VMEM((ITERS, 2, rows, lanes), f32),
            pltpu.VMEM((ITERS, 2, rows, lanes), f32),
            pltpu.VMEM((ITERS, 4, 16, lanes), f32),
            pltpu.VMEM((nx, 1, lanes), f32),
            pltpu.VMEM((ny, 1, lanes), f32),
            pltpu.SemaphoreType.DMA((2,)),
            pltpu.SemaphoreType.REGULAR((max((ny - 2) // 2, 1),)),
            pltpu.SemaphoreType.DMA((2, max(ny, nx))),
            pltpu.SemaphoreType.DMA((2, max(ny, nx))),
            pltpu.SemaphoreType.DMA((ITERS, len(DIRS), 4)),
            pltpu.SemaphoreType.DMA((ITERS, len(DIRS), 4)),
        ],
        compiler_params=pltpu.CompilerParams(
            collective_id=0, has_side_effects=True, vmem_limit_bytes=16 * 2**20
        ),
    )(
        smoothing,
        pltpu.with_memory_space_constraint(volume, pltpu.HBM),
        pltpu.with_memory_space_constraint(tissue_mask, pltpu.HBM),
    )


def solution(mesh):
    placed = (P(None, ("slab", "gy"), "gx"), P(None, ("slab", "gy"), "gx"), P())
    return jax.shard_map(
        on_device,
        mesh=mesh,
        in_specs=placed,
        out_specs=P(None, ("slab", "gy"), "gx"),
        check_vma=False,
    )
```

```python
import functools

import jax
import jax.numpy as jnp
from jax import lax
from jax.experimental import pallas as pl
from jax.experimental.pallas import tpu as pltpu
from jax.sharding import PartitionSpec as P

MESH = pl.DeviceIdType.MESH
ITERS = 2
LOG2E = 1.4426950408889634
BIG = 1e30
DIRS = ((1, 0), (-1, 0), (0, 1), (0, -1), (1, 1), (1, -1), (-1, 1), (-1, -1))
LEVEL = ((0, 0, 8), (0, 8, 8), (0, -8, 8), (0, 8, 0))
CROSS = (
    (4, 0, 8), (4, 8, 8), (4, -8, 8), (-4, 0, 8), (-4, 8, 8), (-4, -8, 8), (4, 0, 0), (4, 8, 0), (4, -8, 0)
)
PAD = 16
SLOTS = 96


def kernel(
    ny, nx, smooth_ref, vol_hbm, mask_hbm, out_ref, vol_ref, mask_ref, mid, vals, packs, squares,
    cubes, totals, band, acc, pcubes, found, pens, ppens, own_tiss, near_tiss, wide_tiss,
    rows_in, row_in, row_out, pack_out, pack_in, corner_in, row_sums, col_sums,
    load_sem, known, sum_send, sum_recv, halo_send, halo_recv,
):
    depth, rows, cols = vol_ref.shape
    lanes = 128
    blocks_z, blocks_y, blocks_x = mask_ref.shape
    nb = rows // 8
    step = lanes - 2
    gy, gx = lax.axis_index("gy"), lax.axis_index("gx")

    barrier = pltpu.get_barrier_semaphore()

    def exists(dy, dx):
        found = None
        for move, pos, count in ((dy, gy, ny), (dx, gx, nx)):
            if move == 0:
                continue
            here = pos < count - move if move > 0 else pos >= -move
            found = here if found is None else jnp.logical_and(found, here)
        return found

    def peer(axis, k):
        pos, count = (gy, ny) if axis == "gy" else (gx, nx)
        return {axis: jnp.where(pos + k >= count, pos + k - count, pos + k)}

    def greet(semaphore, moves):
        for dy, dx in moves:

            @pl.when(exists(dy, dx))
            def _():
                pl.semaphore_signal(
                    semaphore, inc=1, device_id={"gy": gy + dy, "gx": gx + dx}, device_id_type=MESH
                )

    def present(moves):
        return functools.reduce(jnp.add, [exists(dy, dx).astype(jnp.int32) for dy, dx in moves])

    column = [(dy, 0) for dy in (1, -1, 2, -2)]
    others = column + list(DIRS[4:])
    for k in range(1, nx):
        pl.semaphore_signal(barrier, inc=1, device_id=peer("gx", k), device_id_type=MESH)
    greet(barrier, others)

    loads = [
        pltpu.make_async_copy(mask_hbm, mask_ref, load_sem.at[0]),
        pltpu.make_async_copy(vol_hbm, vol_ref, load_sem.at[1]),
    ]
    for load in loads:
        load.start()

    def lane_of(n):
        return lax.broadcasted_iota(jnp.int32, (n, lanes), 1)

    def roll(x, shift):
        shift = shift % lanes
        return pltpu.roll(x, shift, 1) if shift else x

    def packed(planes):
        group = lane_of(planes[0].shape[0]) // 16
        left, right = planes[0][:, 0:lanes], roll(planes[0][:, cols - lanes : cols], 9)
        for z in range(1, depth):
            right = jnp.where(group == z, roll(planes[z][:, cols - lanes : cols], 16 * z + 9), right)
            left = jnp.where(group == z, roll(planes[z][:, 0:lanes], 16 * z), left)
        return left, right

    def packed_line(line):
        match = lane_of(depth) // 16 == lax.broadcasted_iota(jnp.int32, (depth, lanes), 0)
        ends = []
        for at, shift in ((0, 0), (cols - lanes, 9)):
            moved = pltpu.roll(line[:, at : at + lanes], shift, 1, stride=16, stride_axis=0)
            ends.append(jnp.sum(jnp.where(match, moved, 0.0), axis=0, keepdims=True))
        return ends

    def make_packs(src, it):
        for z in range(depth):
            for d, first, ninth in ((0, rows - 1, rows - 9), (1, 0, 8)):
                row_out[it, d, 0, z : z + 1] = src[z, first : first + 1, :]
                row_out[it, d, 1, z : z + 1] = src[z, ninth : ninth + 1, :]
        left, right = packed([src[z] for z in range(depth)])
        pack_out[it, 0] = right
        pack_out[it, 1] = left

    def copies(src, it, d, late):
        dy, dx = DIRS[d]
        pairs = {}
        if late:
            if dx == 0:
                start = rows - 8 if dy > 0 else 0
                pairs[2] = (src.at[:, start : start + 8, :], rows_in.at[it, d])
                pairs[3] = (row_out.at[it, d, 1], row_in.at[it, d, 1])
        elif dx == 0:
            pairs[0] = (row_out.at[it, d, 0], row_in.at[it, d, 0])
        elif dy == 0:
            pairs[0] = (pack_out.at[it, d - 2], pack_in.at[it, d - 2])
        else:
            start = rows - 16 if dy > 0 else 0
            pairs[0] = (pack_out.at[it, 0 if dx > 0 else 1, start : start + 16], corner_in.at[it, d - 4])
        if it == 0 and not late:
            at = {1: slice(cols - lanes, cols), -1: slice(0, lanes), 0: slice(0, cols)}[dx]
            pairs[1] = (own_tiss.at[:, at], near_tiss.at[d, :, at])
        return [
            pltpu.make_async_remote_copy(
                src_ref=a,
                dst_ref=b,
                send_sem=halo_send.at[it, d, j],
                recv_sem=halo_recv.at[it, d, j],
                device_id={"gy": gy + dy, "gx": gx + dx},
                device_id_type=MESH,
            )
            for j, (a, b) in pairs.items()
        ]

    def clear_missing(it):
        for d, (dy, dx) in enumerate(DIRS):

            @pl.when(jnp.logical_not(exists(-dy, -dx)))
            def _():
                if dx == 0:
                    rows_in[it, d] = jnp.zeros(rows_in.shape[2:], jnp.float32)
                    row_in[it, d] = jnp.zeros(row_in.shape[2:], jnp.float32)
                elif dy == 0:
                    pack_in[it, d - 2] = jnp.zeros(pack_in.shape[2:], jnp.float32)
                else:
                    corner_in[it, d - 4] = jnp.zeros(corner_in.shape[2:], jnp.float32)
                if it == 0:
                    near_tiss[d] = jnp.zeros(near_tiss.shape[1:], jnp.float32)

    def start_halo(src, it):
        for late in (False, True):
            for d, (dy, dx) in enumerate(DIRS[:2] if late else DIRS):

                @pl.when(exists(dy, dx))
                def _():
                    for copy in copies(src, it, d, late):
                        copy.start()

    def wait_halo(src, it, late):
        for d, (dy, dx) in enumerate(DIRS[:2] if late else DIRS):

            @pl.when(exists(-dy, -dx))
            def _():
                for copy in copies(src, it, d, late):
                    copy.wait_recv()

    def wait_sent(src, it):
        for d, (dy, dx) in enumerate(DIRS):

            @pl.when(exists(dy, dx))
            def _():
                for late in (False, True):
                    for copy in copies(src, it, d, late):
                        copy.wait_send()

    def sum_copies(axis):
        count, buffer = (nx, row_sums) if axis == "gx" else (ny, col_sums)
        stage = 0 if axis == "gx" else 1
        return [
            pltpu.make_async_remote_copy(
                src_ref=buffer.at[0],
                dst_ref=buffer.at[k],
                send_sem=sum_send.at[stage, k],
                recv_sem=sum_recv.at[stage, k],
                device_id=peer(axis, k),
                device_id_type=MESH,
            )
            for k in range(1, count)
        ]

    def spread(ref, index, flags):
        for k in range(nb + 2):
            ref[index + (slice(8 * k, 8 * k + 8),)] = jnp.broadcast_to(flags[k : k + 1], (8, lanes))

    def spread_tissue():
        lane = lane_of(8)
        spot = lane % 16
        inner = jnp.logical_and(lane > 0, lane < lanes - 1)
        valid = jnp.logical_or(
            jnp.logical_and(spot >= 1, spot <= 9), jnp.logical_and(spot >= 12, spot <= 14)
        )
        patterns = {}
        for zb in range(blocks_z):
            first = zb * blocks_y
            wide_tiss[zb, 1 : 1 + blocks_y, lanes : lanes + cols] = own_tiss[first : first + blocks_y]
            wide_tiss[zb, 1 : 1 + blocks_y, 0:lanes] = near_tiss[2, first : first + blocks_y, cols - lanes : cols]
            wide_tiss[zb, 1 : 1 + blocks_y, lanes + cols :] = near_tiss[3, first : first + blocks_y, 0:lanes]
            for row, source, at in ((0, (0, 4, 5), first + blocks_y - 1), (1 + blocks_y, (1, 6, 7), first)):
                mid_d, left_d, right_d = source
                wide_tiss[zb, row : row + 1, lanes : lanes + cols] = near_tiss[mid_d, at : at + 1, :]
                wide_tiss[zb, row : row + 1, 0:lanes] = near_tiss[left_d, at : at + 1, cols - lanes : cols]
                wide_tiss[zb, row : row + 1, lanes + cols :] = near_tiss[right_d, at : at + 1, 0:lanes]
            for ci in range(2):
                c = 8 * ci
                for t in range(2):
                    off = lanes + step * t + c
                    flags = (wide_tiss[zb, 0:8, off : off + lanes] - 1.0) * BIG
                    if ci == 0:
                        flags = jnp.where(inner, flags, -BIG)
                    spread(pens, (ci, t, zb), flags)
                left = wide_tiss[zb, 0:8, lanes - 9 + c : 2 * lanes - 9 + c]
                off = lanes + 2 * step + c - 11
                right = wide_tiss[zb, 0:8, off : off + lanes]
                part = jnp.where(lane < 11, left, jnp.where(lane < 16, right, 0.0))
                for shift in (16, 32, 64):
                    part = part + roll(part, shift)
                patterns[zb, ci] = (part - 1.0) * BIG
        low = lane < lanes // 2
        both = [jnp.where(low, patterns[0, ci], patterns[1, ci]) for ci in range(2)]
        own = jnp.where(valid, both[0], -BIG)
        spread(ppens, (0,), own)
        spread(ppens, (1,), both[1])
        spread(ppens, (2,), jnp.where(low, own, -BIG))
        spread(ppens, (3,), patterns[1, 0])
        spread(ppens, (4,), patterns[1, 1])
        spread(ppens, (5,), jnp.where(low, -BIG, own))
        spread(ppens, (6,), patterns[0, 1])
        spread(ppens, (7,), patterns[0, 0])

    def shifted(n0, n1, extra):
        lane = lane_of(n0.shape[0])
        return (
            n0,
            jnp.where(lane < 2, roll(n0, 2), roll(n1, 2)),
            jnp.where(lane < lanes - 8, roll(n0, -8), roll(n1, -8)),
            roll(n1, -6) if extra is None else jnp.where(lane < lanes - 6, roll(n1, -6), extra),
        )

    def fill_own(src):
        for z in range(depth):
            four = shifted(src[z, :, 0:lanes], src[z, :, lanes : 2 * lanes], None)
            for k, part in enumerate(four):
                vals[k // 2, k % 2, z, PAD : PAD + rows] = part

    def fill_line(it, d, which, corner, at):
        line = jnp.broadcast_to(corner_in[it, 2 * d + 1, corner : corner + 1], (depth, lanes))
        extra = pltpu.roll(line, 10, 1, stride=16, stride_axis=0)
        single = row_in[it, d, which]
        four = shifted(single[:, 0:lanes], single[:, lanes : 2 * lanes], None)
        for k, part in enumerate(four):
            for z in range(depth):
                row = part[z : z + 1]
                if k == 3:
                    row = jnp.where(lane_of(1) < lanes - 6, row, extra[depth - 1 - z : depth - z])
                vals[k // 2, k % 2, z, at : at + 1] = row
        fill_packs(
            at, corner_in[it, 2 * d, corner : corner + 1], packed_line(single),
            corner_in[it, 2 * d + 1, corner : corner + 1],
        )

    def fill_early(it):
        lane = lane_of(rows)
        for z in range(depth):
            extra = roll(pack_in[it, 1], lanes - 6 - 16 * z)
            vals[1, 1, z, PAD : PAD + rows] = jnp.where(
                lane < lanes - 6, vals[1, 1, z, PAD : PAD + rows], extra
            )
        fill_packs(PAD, pack_in[it, 0], (pack_out[it, 1], pack_out[it, 0]), pack_in[it, 1])
        fill_line(it, 0, 0, 15, PAD - 1)
        fill_line(it, 1, 0, 0, PAD + rows)
        fill_squares()

    def fill_late(it):
        for d, at, single, alone in ((0, 8, 7, PAD - 9), (1, 0, 8, PAD + rows + 8)):
            start = PAD - 8 if d == 0 else PAD + rows
            for z in range(depth):
                extra = roll(corner_in[it, 2 * d + 1, at : at + 8], lanes - 6 - 16 * z)
                four = shifted(rows_in[it, d, z, :, 0:lanes], rows_in[it, d, z, :, lanes : 2 * lanes], extra)
                for k, part in enumerate(four):
                    vals[k // 2, k % 2, z, start : start + 8] = part
            fill_line(it, d, 1, single, alone)
            fill_packs(
                start, corner_in[it, 2 * d, at : at + 8], packed([rows_in[it, d, z] for z in range(depth)]),
                corner_in[it, 2 * d + 1, at : at + 8],
            )
        fill_squares()

    def fill_packs(start, right_of_left, own, left_of_right):
        left, right = own
        size = left.shape[0]
        lane = lane_of(size)
        spot, group = lane % 16, lane // 16
        zero = jnp.where(
            spot < 9,
            right_of_left,
            jnp.where(
                spot < 11, roll(left, 9), jnp.where(spot < 15, roll(right, 6), roll(left_of_right, 15))
            ),
        )
        eight = jnp.where(
            spot < 1, roll(right_of_left, -8), jnp.where(spot < 11, roll(left, 1), roll(left_of_right, 7))
        )
        hole = jnp.logical_and(group >= 4, group < 7)
        gap = jnp.logical_and(group >= 1, group < 4)
        half_zero, half_eight = roll(zero, 64), roll(eight, 64)
        at = slice(start, start + size)
        packs[0, at] = zero
        packs[1, at] = eight
        packs[2, at] = jnp.where(group == 7, 0.0, zero)
        packs[3, at] = jnp.where(hole, 0.0, half_zero)
        packs[4, at] = jnp.where(hole, 0.0, half_eight)
        packs[5, at] = jnp.where(group == 0, 0.0, zero)
        packs[6, at] = jnp.where(gap, 0.0, half_eight)

    def fill_squares():
        for t in range(2):
            for ci in range(2):
                for k in range(2):
                    plane = vals[ci, t, depth // 2 - 1 + k]
                    squares[k, ci, t] = plane * plane

    def extent(b):
        k0 = -1 if b > 0 else 0
        k1 = nb + 1 if b < 0 else nb
        return k0, k1, PAD + 8 * (k0 - 1), 8 * (k1 - k0 + 2)

    def add(ref, index, value, init):
        ref[index] = value if init else ref[index] + value

    def box(parts, kind=0):
        tops = [part.astype(jnp.bfloat16).astype(jnp.float32) for part in parts]
        lhs = [jnp.concatenate([top, part - top], axis=1) for part, top in zip(parts, tops)]
        return jnp.dot(jnp.concatenate(lhs, axis=0), band[kind], preferred_element_type=jnp.float32)

    def main_offset(t, offset, init, scale, slot, mode):
        a, b, c = offset
        ci, bb = c // 8, b // 8
        k0, k1, lo, size = extent(b)
        inner = size - 16
        low, planes = max(0, -a), depth - abs(a)
        high = low + planes

        def differ(z, low_row, count):
            far = slice(low_row + b, low_row + b + count)
            return vals[ci, t, z + a, far] - vals[0, t, z, low_row : low_row + count]

        def outside(z):
            if a == 0:
                return None
            if (z < low) == (a > 0):
                return squares[0 if a > 0 else 1, ci, t, lo + b : lo + b + size]
            return squares[1 if a > 0 else 0, 0, t, lo : lo + size]

        own_pen, far_pen = slice(8 * (k0 + 1), 8 * (k1 + 1)), slice(8 * (k0 + bb + 1), 8 * (k1 + bb + 1))
        po, qo = -8 * k0, -8 * (bb + k0)
        penalty = None
        before = None
        diffs, sqs = {}, {}
        queue = []

        def grow(z):
            diffs[z] = differ(z, lo, size)
            sqs[z] = diffs[z] * diffs[z]

        if mode != "apply":
            before = outside(low - 1)
            grow(low)
        for z in range(low, high, 2):
            if z % 4 == 0 and mode != "measure":
                penalty = pens[0, t, z // 4, own_pen] + pens[ci, t, (z + a) // 4, far_pen]
            cubed = (None, None)
            if mode != "apply":
                grow(z + 1)
                pair = sqs[z] + sqs[z + 1]
                if z + 2 < high:
                    grow(z + 2)
                    after = sqs[z + 2]
                else:
                    after = outside(high)
                cubed = (
                    pair if before is None else pair + before,
                    pair if after is None else pair + after,
                )
                before = sqs[z + 1]
            for plane, cube in zip((z, z + 1), cubed):
                if mode != "apply":
                    at = slot % SLOTS
                    cubes[at, 0:size] = cube
                    total = cube[8 : 8 + inner] + cubes[at, 7 : 7 + inner] + cubes[at, 9 : 9 + inner]
                    if mode == "measure":
                        slot += 1
                        queue.append(total)
                        continue
                    total = total + roll(total, 1) + roll(total, -1)
                if mode == "apply":
                    total = totals[t, slot, 0:inner]
                    gap = differ(plane, lo + 8, inner)
                else:
                    gap = diffs[plane][8 : 8 + inner]
                slot += 1
                weight = jnp.exp2(penalty - (total if scale is None else total * scale[0:inner]))
                push = weight * gap
                add(acc, (0, 0, t, plane), push[po : po + rows], init)
                add(acc, (0, 1, t, plane), weight[po : po + rows], init)
                far = plane + a
                if init:
                    acc[ci, 0, t, far] = -push[qo : qo + rows]
                else:
                    acc[ci, 0, t, far] -= push[qo : qo + rows]
                add(acc, (ci, 1, t, far), weight[qo : qo + rows], init)
        if mode == "measure":
            summed = box(queue)
            for k in range(len(queue)):
                totals[t, slot - len(queue) + k, 0:inner] = summed[k * inner : (k + 1) * inner]
        return slot

    order = [offset for offset in LEVEL + CROSS if offset[1] == 0]
    flat = len(order)
    order += [offset for offset in LEVEL + CROSS if offset[1] != 0]
    bases = [sum(depth - abs(other[0]) for other in order[:k]) for k in range(len(order))]

    def main_gather(jobs, scale, mode):
        def body(t, carry):
            for k in jobs:
                if mode == "both" and k in (2, 5, 8, 11):
                    main_offset(t, order[k], k == 0, None, bases[k], "measure")
                    main_offset(t, order[k], k == 0, None, bases[k], "apply")
                else:
                    main_offset(t, order[k], k == 0, scale, bases[k], mode)
            return carry

        lax.fori_loop(0, 2, body, 0)

    packed_items = []
    for a, b, c in LEVEL + CROSS:
        near, far = {0: (0, c // 8), 4: (2, 3 + c // 8), -4: (5, 6)}[a]
        packed_items.append((near, far, b, c // 8 + 2 * (a != 0), a == 0))

    def pack_differ(near, far, b, low, size):
        return packs[far, low + b : low + b + size] - packs[near, low : low + size]

    def pack_measure():
        for k, (near, far, b, key, masked) in enumerate(packed_items):
            lo, size = extent(b)[2:]
            gap = pack_differ(near, far, b, lo, size)
            pcubes[k, 0:size] = gap * gap
        for kind in range(2):
            chosen = [(k, item) for k, item in enumerate(packed_items) if item[4] == (kind == 0)]
            parts = []
            for k, item in chosen:
                inner = extent(item[2])[3] - 16
                parts.append(pcubes[k, 7 : 7 + inner] + pcubes[k, 8 : 8 + inner] + pcubes[k, 9 : 9 + inner])
            pooled = box(parts, 1 + kind)
            at = 0
            for (k, item), part in zip(chosen, parts):
                found[k, 0 : part.shape[0]] = pooled[at : at + part.shape[0]]
                at += part.shape[0]

    def pack_apply(scale):
        parts = [[None] * 4, [None] * 4]

        def gain(kind, key, value, minus):
            old = parts[kind][key]
            if old is None:
                parts[kind][key] = -value if minus else value
            else:
                parts[kind][key] = old - value if minus else old + value

        for k, (near, far, b, key, masked) in enumerate(packed_items):
            k0, k1, lo, size = extent(b)
            bb, inner = b // 8, size - 16
            penalty = ppens[near, 8 * (k0 + 1) : 8 * (k1 + 1)] + ppens[far, 8 * (k0 + bb + 1) : 8 * (k1 + bb + 1)]
            total = found[k, 0:inner]
            weight = jnp.exp2(penalty - (total if scale is None else total * scale[0:inner]))
            push = weight * pack_differ(near, far, b, lo + 8, inner)
            po, qo = -8 * k0, -8 * (bb + k0)
            gain(0, 0, push[po : po + rows], False)
            gain(1, 0, weight[po : po + rows], False)
            gain(0, key, push[qo : qo + rows], True)
            gain(1, key, weight[qo : qo + rows], False)
        return parts

    def merge(parts):
        lane = lane_of(rows)
        spot = lane % 16
        merged = []
        for kind in range(2):
            zero = parts[kind][0] + roll(parts[kind][2], 64)
            eight = parts[kind][1] + roll(parts[kind][3], 64)
            eight = eight + jnp.where(spot == 1, roll(zero, -8), 0.0)
            merged.append(
                jnp.where(jnp.logical_or(spot >= 14, spot == 0), roll(zero, -14), jnp.where(spot < 10, eight, 0.0))
            )
        return merged

    def finish(src, dst, merged, factor):
        lane = lane_of(rows)
        for z in range(depth):
            sides = []
            for kind in range(2):
                near = roll(merged[kind], -(16 * z + 1))
                first = acc[0, kind, 0, z]
                second = roll(acc[0, kind, 1, z], -2)
                far_first = roll(acc[1, kind, 0, z], 8)
                far_second = roll(acc[1, kind, 1, z], 6)
                sides.append((
                    first + jnp.where(lane < 9, near, far_first) + jnp.where(lane == lanes - 1, second, 0.0),
                    jnp.where(lane >= lanes - 3, near, second) + jnp.where(lane < 7, far_first, far_second),
                ))
            for t in range(2):
                at = slice(t * lanes, (t + 1) * lanes)
                dst[z, :, at] = (src[z, :, at] + sides[0][t] / (sides[1][t] + 1.0)) * factor

    row_at = lax.broadcasted_iota(jnp.int32, (2 * lanes, lanes), 0) % lanes
    col_at = lax.broadcasted_iota(jnp.int32, (2 * lanes, lanes), 1)
    beside = jnp.abs(row_at % 16 - col_at % 16) <= 1
    apart = jnp.abs(row_at // 16 - col_at // 16)
    for kind, rule in enumerate((
        jnp.abs(row_at - col_at) <= 1,
        jnp.logical_and(beside, apart <= 1),
        jnp.logical_and(beside, jnp.logical_or(apart <= 1, apart == depth - 1)),
    )):
        band[kind] = rule.astype(jnp.float32)
    loads[0].wait()
    widen = (
        lax.broadcasted_iota(jnp.int32, (blocks_x, cols), 1) // 8
        == lax.broadcasted_iota(jnp.int32, (blocks_x, cols), 0)
    ).astype(jnp.float32)
    for zb in range(blocks_z):
        flags = mask_ref[zb].astype(jnp.float32)
        own_tiss[zb * blocks_y : (zb + 1) * blocks_y] = jnp.dot(
            flags, widen, preferred_element_type=jnp.float32
        )
    loads[1].wait()
    total = jnp.zeros((8, cols), jnp.float32)
    count = jnp.zeros((8, cols), jnp.float32)
    for z in range(1, depth - 1):
        residual = vol_ref[z] - 0.5 * (vol_ref[z - 1] + vol_ref[z + 1])
        for yb in range(blocks_y):
            line = (z // 4) * blocks_y + yb
            flag = jnp.broadcast_to(own_tiss[line : line + 1], (8, cols))
            piece = residual[8 * yb : 8 * yb + 8]
            total = total + flag * piece * piece
            count = count + flag
    total = jnp.sum(total, axis=0, keepdims=True)
    count = jnp.sum(count, axis=0, keepdims=True)
    tiles = cols // lanes
    total = functools.reduce(jnp.add, [total[:, i * lanes : (i + 1) * lanes] for i in range(tiles)])
    count = functools.reduce(jnp.add, [count[:, i * lanes : (i + 1) * lanes] for i in range(tiles)])
    lane = lax.broadcasted_iota(jnp.int32, (1, lanes), 1)
    row_sums[0] = jnp.where(
        lane < lanes // 2,
        jnp.sum(total, axis=1, keepdims=True),
        jnp.sum(count, axis=1, keepdims=True),
    )
    make_packs(vol_ref, 0)
    pl.semaphore_wait(barrier, nx - 1 + present(others))
    rounds = known.shape[0]
    for copy in sum_copies("gx"):
        copy.start()
    greet(known.at[0], column)
    start_halo(vol_ref, 0)
    for it in range(ITERS):
        clear_missing(it)
    fill_own(vol_ref)
    for k in range(rounds):
        pl.semaphore_wait(known.at[k], present(column))
        if k + 1 < rounds:
            greet(known.at[k + 1], column)
    for copy in sum_copies("gx"):
        copy.wait_recv()
    col_sums[0] = functools.reduce(jnp.add, [row_sums[k] for k in range(nx)])
    for copy in sum_copies("gy"):
        copy.start()
    wait_halo(vol_ref, 0, False)
    spread_tissue()
    fill_early(0)
    main_gather(range(flat), None, "measure")
    wait_halo(vol_ref, 0, True)
    fill_late(0)
    pack_measure()
    main_gather(range(flat, len(order)), None, "measure")
    for copy in sum_copies("gy"):
        copy.wait_recv()
    everything = functools.reduce(jnp.add, [col_sums[k] for k in range(ny)])
    summed = everything[:, 0:1] * (2.0 / 3.0)
    tissue_count = everything[:, lanes // 2 : lanes // 2 + 1]
    variance = summed / jnp.maximum(tissue_count, 1.0) + 1e-05
    width = 54.0 * smooth_ref[0] * smooth_ref[0]
    power = LOG2E / (width * variance)
    scale = jnp.broadcast_to(power, (rows + 8, lanes))
    root = jnp.broadcast_to(jnp.sqrt(power), (rows, lanes))
    inverse = jnp.broadcast_to(1.0 / jnp.sqrt(power), (rows, lanes))
    merged = merge(pack_apply(scale))
    main_gather(range(len(order)), scale, "apply")
    finish(vol_ref, mid, merged, root)
    make_packs(mid, 1)
    start_halo(mid, 1)
    fill_own(mid)
    wait_halo(mid, 1, False)
    fill_early(1)
    main_gather(range(flat), None, "both")
    wait_halo(mid, 1, True)
    fill_late(1)
    pack_measure()
    merged = merge(pack_apply(None))
    main_gather(range(flat, len(order)), None, "both")
    finish(mid, out_ref, merged, inverse)
    wait_sent(vol_ref, 0)
    wait_sent(mid, 1)
    for axis in ("gx", "gy"):
        for copy in sum_copies(axis):
            copy.wait_send()


def on_device(volume, tissue_mask, smoothing):
    ny, nx = lax.axis_size("gy"), lax.axis_size("gx")
    depth, rows, cols = volume.shape
    blocks_z, blocks_y, blocks_x = tissue_mask.shape
    lanes = 128
    assert depth == 8 and cols == 2 * lanes and blocks_z == 2
    flag_rows = -(-(blocks_y + 2) // 8) * 8
    f32 = jnp.float32
    vmem = pl.BlockSpec(memory_space=pltpu.VMEM)
    anywhere = pl.BlockSpec(memory_space=pltpu.HBM)
    return pl.pallas_call(
        functools.partial(kernel, ny, nx),
        out_shape=jax.ShapeDtypeStruct(volume.shape, f32),
        in_specs=[pl.BlockSpec(memory_space=pltpu.SMEM), anywhere, anywhere],
        out_specs=vmem,
        scratch_shapes=[
            pltpu.VMEM((depth, rows, cols), f32),
            pltpu.VMEM((blocks_z, blocks_y, blocks_x), jnp.int32),
            pltpu.VMEM((depth, rows, cols), f32),
            pltpu.VMEM((2, 2, depth, rows + 2 * PAD, lanes), f32),
            pltpu.VMEM((7, rows + 2 * PAD, lanes), f32),
            pltpu.VMEM((2, 2, 2, rows + 2 * PAD, lanes), f32),
            pltpu.VMEM((SLOTS, rows + 24, lanes), f32),
            pltpu.VMEM((2, len(LEVEL) * depth + len(CROSS) * depth // 2, rows + 8, lanes), f32),
            pltpu.VMEM((3, 2 * lanes, lanes), f32),
            pltpu.VMEM((2, 2, 2, depth, rows, lanes), f32),
            pltpu.VMEM((13, rows + 24, lanes), f32),
            pltpu.VMEM((13, rows + 8, lanes), f32),
            pltpu.VMEM((2, 2, blocks_z, rows + 16, lanes), f32),
            pltpu.VMEM((8, rows + 16, lanes), f32),
            pltpu.VMEM((blocks_z * blocks_y, cols), f32),
            pltpu.VMEM((len(DIRS), blocks_z * blocks_y, cols), f32),
            pltpu.VMEM((blocks_z, flag_rows, cols + 2 * lanes), f32),
            pltpu.VMEM((ITERS, 2, depth, 8, cols), f32),
            pltpu.VMEM((ITERS, 2, 2, depth, cols), f32),
            pltpu.VMEM((ITERS, 2, 2, depth, cols), f32),
            pltpu.VMEM((ITERS, 2, rows, lanes), f32),
            pltpu.VMEM((ITERS, 2, rows, lanes), f32),
            pltpu.VMEM((ITERS, 4, 16, lanes), f32),
            pltpu.VMEM((nx, 1, lanes), f32),
            pltpu.VMEM((ny, 1, lanes), f32),
            pltpu.SemaphoreType.DMA((2,)),
            pltpu.SemaphoreType.REGULAR((max((ny - 2) // 2, 1),)),
            pltpu.SemaphoreType.DMA((2, max(ny, nx))),
            pltpu.SemaphoreType.DMA((2, max(ny, nx))),
            pltpu.SemaphoreType.DMA((ITERS, len(DIRS), 4)),
            pltpu.SemaphoreType.DMA((ITERS, len(DIRS), 4)),
        ],
        compiler_params=pltpu.CompilerParams(
            collective_id=0, has_side_effects=True, vmem_limit_bytes=16 * 2**20
        ),
    )(
        smoothing,
        pltpu.with_memory_space_constraint(volume, pltpu.HBM),
        pltpu.with_memory_space_constraint(tissue_mask, pltpu.HBM),
    )


def solution(mesh):
    placed = (P(None, ("slab", "gy"), "gx"), P(None, ("slab", "gy"), "gx"), P())
    return jax.shard_map(
        on_device,
        mesh=mesh,
        in_specs=placed,
        out_specs=P(None, ("slab", "gy"), "gx"),
        check_vma=False,
    )
```
